768 devices in a mesh: lat: 16 (over z_hi, x), lon: 48 (over z_lo, y, core).
Axes of the slice: x: 4, y: 8, z: 12 (z_hi: 4, z_lo: 3; z = z_hi * 3 + z_lo), core: 2. Of those that a mesh axis runs over, the one named last changes fastest.
Arguments:
- ensemble: bfloat16 [192, 128, 10240], P('lon', 'lat'), may hold values from -0.625 to 0.625
- innovation: float32 [384, 256, 128], P('lon', 'lat'), may hold values from -6 to 6
- obs_weight: float32 [384, 256, 128], P('lon', 'lat'), may hold values from 0.5 to 20
- lat_offset: int32 [256], P('lat'), may hold values from 0 to 3
- lat_weight: float32 [256], P('lat'), may hold values from 0 to 1
- band_widths: int32 [80], replicated, may hold values from 1 to 63
Outputs:
- coefficients: float32 [2, 2], replicated
- next_vector: bfloat16 [192, 128, 5120], P('lon', 'lat')
The draws below stay inside these ranges and needn't reach their ends.
All inputs are finite; a program needn't handle non-finite values.
Results may differ from the reference program's by a relative error of at most 0.0014.
Values sent between devices are 32-bit elements; how exact they have to be, the bound alone decides.
A program may use at most 32 MiB of HBM per device.

```python
import math
import jax
import jax.numpy as jnp
from jax import lax

M = 80
LEV = 64
FIELDS = 2
ITERS = 2
NCLAT = 128
NCLON = 192
NFLAT = 256
NFLON = 384


def with_ends(drawn, own_key, least, largest):
    place = [jax.random.randint(jax.random.fold_in(own_key, axis), (), 0, length) for axis, length in enumerate(drawn.shape)]
    widest = drawn.shape.index(max(drawn.shape))
    neighbour = place[:widest] + [(place[widest] + 1) % drawn.shape[widest]] + place[widest + 1:]
    return drawn.at[tuple(place)].set(least).at[tuple(neighbour)].set(largest)


def block_scale(rng, shape, shards, low, high):
    level = 1.0
    for position, blocks in shards:
        steps = jax.random.uniform(jax.random.fold_in(jax.random.fold_in(rng, 6), position), (blocks,), jnp.float32, low / len(shards), high / len(shards))
        level = level * jnp.repeat(jnp.exp(steps), shape[position] // blocks).reshape((-1,) + (1,) * (len(shape) - 1 - position))
    return level


def bell_draw(key, shape, deviation, limit, cuts=(), held_as=jnp.bfloat16):
    level = block_scale(key, shape, cuts, -0.22, 0.18) if cuts else 1.0
    array = jax.random.normal(key, shape, jnp.float32) * deviation * level
    return jnp.minimum(jnp.maximum(array, -limit), limit).astype(held_as)


def setup_inputs(seed: int = 0) -> dict:
    streams_of = jax.random.split(jax.random.key(seed), 7)
    ensemble = bell_draw(streams_of[0], (NCLON, NCLAT, M * FIELDS * LEV), M ** -0.5, 0.625, ((0, 48), (1, 16)))
    innovation = bell_draw(streams_of[1], (NFLON, NFLAT, FIELDS * LEV), 1.0, 6.0, ((0, 48), (1, 16)), jnp.float32)
    obs_weight = jnp.clip(jnp.exp(math.log(20.0) - 3.6888795 * jax.random.uniform(streams_of[2], (NFLON, NFLAT, FIELDS * LEV), jnp.float32) ** block_scale(streams_of[2], (NFLON, NFLAT, FIELDS * LEV), ((0, 48), (1, 16)), -0.2, 0.2)), 0.5, 20.0)
    lat_offset = with_ends(jax.random.randint(streams_of[3], (NFLAT,), 0, 4), jax.random.fold_in(streams_of[3], 1), 0, 3).astype(jnp.int32)
    lat_weight = jnp.clip(1.0 * jax.random.uniform(streams_of[4], (NFLAT,), jnp.float32) ** block_scale(streams_of[4], (NFLAT,), ((0, 16),), -0.2, 0.2), 0.0, 1.0)
    band_widths = with_ends(jax.random.randint(streams_of[5], (M,), 1, LEV), jax.random.fold_in(streams_of[5], 1), 1, LEV - 1).astype(jnp.int32)
    return dict(ensemble=ensemble, innovation=innovation, obs_weight=obs_weight, lat_offset=lat_offset, lat_weight=lat_weight, band_widths=band_widths)


EVEN_TAPS = (-0.0234375, 0.2265625, 0.8671875, -0.0703125)
ODD_TAPS = (-0.0703125, 0.8671875, 0.2265625, -0.0234375)
EPSILON = 1e-06

def tent_matrix(band_widths, levels):
    level_ids = jnp.arange(levels, dtype=jnp.int32)
    distance = jnp.abs(level_ids[:, None] - level_ids[None, :]).astype(jnp.float32)
    widths = (band_widths + 1).astype(jnp.float32)[:, None, None]
    return jnp.maximum(0.0, 1.0 - distance[None] / widths) / widths

def tap_sum(padded, taps, first, length):
    result = taps[0] * padded[first:first + length]
    for offset in range(1, 4):
        result = result + taps[offset] * padded[first + offset:first + offset + length]
    return result

def fold_taps(padded, taps, first, length):
    result = taps[0] * padded[first:first + 2 * length:2]
    for offset in range(1, 4):
        start_at = first - 2 * offset
        result = result + taps[offset] * padded[start_at:start_at + 2 * length:2]
    return result

def localize_rows(values, tent):
    shaped = values.reshape(values.shape[0], M, LEV)
    mapped = jnp.einsum('aml,mlk->amk', shaped, tent, precision=lax.Precision.HIGHEST)
    return mapped.reshape(values.shape[0], M * LEV)

def reference(ensemble, innovation, obs_weight, lat_offset, lat_weight, band_widths):
    tent = tent_matrix(band_widths, LEV)
    fine_rows = jnp.arange(NFLAT, dtype=jnp.int32)
    lower = fine_rows // 2 - 2 + lat_offset
    columns = jnp.arange(NCLAT, dtype=jnp.int32)
    interp = (1.0 - lat_weight)[:, None] * (columns[None, :] == lower[:, None]) + lat_weight[:, None] * (columns[None, :] == lower[:, None] + 1)
    entries = float(NCLON * NCLAT * M * LEV)

    def combine(vector):

        def one_column(pieces):
            ens_col, vec_col = pieces
            weights = localize_rows(vec_col, tent)
            shaped = ens_col.astype(jnp.float32).reshape(NCLAT, M, FIELDS, LEV)
            summed = lax.optimization_barrier(jnp.sum(shaped * weights.reshape(NCLAT, M, 1, LEV), axis=1))
            return summed.reshape(NCLAT, FIELDS * LEV)
        return lax.map(one_column, (ensemble, vector))

    def spread(coarse):

        def one_column(pieces):
            ens_col, grad_col = pieces
            shaped = ens_col.astype(jnp.float32).reshape(NCLAT, M, FIELDS, LEV)
            summed = lax.optimization_barrier(jnp.sum(shaped * grad_col.reshape(NCLAT, 1, FIELDS, LEV), axis=2))
            return localize_rows(summed.reshape(NCLAT, M * LEV), tent)
        return lax.map(one_column, (ensemble, coarse))

    def prolong(increment):
        fine_lat = jnp.einsum('ri,cil->crl', interp, increment, precision=lax.Precision.HIGHEST)
        padded = jnp.concatenate([fine_lat[-2:], fine_lat, fine_lat[:2]], axis=0)
        even_cols = tap_sum(padded, EVEN_TAPS, 0, NCLON)
        odd_cols = tap_sum(padded, ODD_TAPS, 1, NCLON)
        return jnp.stack([even_cols, odd_cols], axis=1).reshape(NFLON, NFLAT, FIELDS * LEV)

    def restrict(fine):
        padded = jnp.concatenate([fine[-3:], fine, fine[:3]], axis=0)
        coarse_lon = fold_taps(padded, EVEN_TAPS, 7, NCLON) + fold_taps(padded, ODD_TAPS, 6, NCLON)
        return jnp.einsum('ri,crl->cil', interp, coarse_lon, precision=lax.Precision.HIGHEST)

    def hessian(vector):
        return vector + spread(restrict(obs_weight * prolong(combine(vector))))
    current = spread(restrict(obs_weight * innovation))
    basis = []
    diagonal = []
    off_diagonal = []
    for step in range(ITERS):
        norm_value = jnp.sqrt(jnp.sum(current * current) / entries + EPSILON)
        normed = current / norm_value
        image = hessian(normed)
        basis.append(normed)
        dots = [jnp.sum(member * image) / entries for member in basis]
        for member, weight in zip(basis, dots):
            image = image - weight * member
        diagonal.append(dots[-1])
        off_diagonal.append(norm_value)
        current = image
    coefficients = jnp.stack([jnp.stack(diagonal), jnp.stack(off_diagonal)]).astype(jnp.float32)
    return (coefficients, current.astype(jnp.bfloat16))
```

```python
import functools

import jax
import jax.numpy as jnp
from jax import lax
from jax.experimental import pallas as pl
from jax.experimental.pallas import tpu as pltpu
from jax.sharding import PartitionSpec as P

M = 80
LEV = 64
PAIRS = M // 2
EVEN_TAPS = (-0.0234375, 0.2265625, 0.8671875, -0.0703125)
ODD_TAPS = (-0.0703125, 0.8671875, 0.2265625, -0.0234375)
EPSILON = 1e-06
F32 = jnp.float32
BF16 = jnp.bfloat16
MESH = pl.DeviceIdType.MESH
TOPO = (4, 4, 3, 8, 2)
DIRECTIONS = ((1, 1), (1, -1), (-1, 1), (-1, -1), (1, 0), (-1, 0), (0, 1), (0, -1))
UNROLL = 4


def kernel(
    topo,
    entries,
    ens_hbm,
    innov_hbm,
    wobs_hbm,
    offset_ref,
    weight_ref,
    bands_ref,
    coef_out,
    vec_out,
    ens,
    dext,
    wext,
    wsplit,
    zext,
    yv,
    params,
    coef,
    gbuf,
    tents,
    sq_hi,
    sq_lo,
    inv2,
    uvec,
    red_a,
    red_b,
    red_c,
    local_sem,
    in_send,
    in_recv,
    par_send,
    par_recv,
    z_send,
    z_recv,
    a_send,
    a_recv,
    b_send,
    b_recv,
    c_send,
    c_recv,
):
    zh_n, x_n, zl_n, y_n, core_n = topo
    lat_n, lon_n = zh_n * x_n, zl_n * y_n * core_n
    lat, lon = lax.axis_index("lat"), lax.axis_index("lon")
    z_hi, x = lat // x_n, lat % x_n
    z_lo, y_core = lon // (y_n * core_n), lon % (y_n * core_n)
    y_pos, core = y_core // core_n, y_core % core_n

    def neighbour(dlat, dlon):
        return (lat + dlat, lax.rem(lon + dlon + lon_n, lon_n))

    def inside(dlat, body):
        if dlat == 0:
            body()
        else:
            pl.when((lat + dlat >= 0) & (lat + dlat < lat_n))(body)

    def dev_a(i):
        return (z_hi * x_n + i // core_n, lon - core + i % core_n)

    def dev_b(i):
        return (lat, z_lo * (y_n * core_n) + i * core_n + core)

    def dev_c(i):
        return ((i // zl_n) * x_n + x, (i % zl_n) * (y_n * core_n) + y_core)

    stages = (
        (x * core_n + core, x_n * core_n, dev_a, red_a, a_send, a_recv),
        (y_pos, y_n, dev_b, red_b, b_send, b_recv),
        (z_hi * zl_n + z_lo, zh_n * zl_n, dev_c, red_c, c_send, c_recv),
    )

    dext[...] = jnp.zeros(dext.shape, F32)
    wext[...] = jnp.zeros(wext.shape, F32)
    zext[...] = jnp.zeros(zext.shape, F32)
    params[...] = jnp.zeros(params.shape, F32)
    params[1, 0:1, 0:16] = weight_ref[...]
    params[1, 1:2, 0:16] = offset_ref[...].astype(F32)

    barrier = pltpu.get_barrier_semaphore()
    for dlat, dlon in DIRECTIONS:

        def greet(dlat=dlat, dlon=dlon):
            pl.semaphore_signal(
                barrier, inc=1, device_id=neighbour(dlat, dlon), device_id_type=MESH
            )

        inside(dlat, greet)
    for me, count, device, _, _, _ in stages:
        for step in range(1, count):
            pl.semaphore_signal(
                barrier,
                inc=1,
                device_id=device(lax.rem(me + step, count)),
                device_id_type=MESH,
            )

    own_d = pltpu.make_async_copy(innov_hbm, dext.at[3:11, 8:24], local_sem.at[0])
    own_w = pltpu.make_async_copy(wobs_hbm, wext.at[3:11, 8:24], local_sem.at[1])
    own_e = pltpu.make_async_copy(ens_hbm, ens, local_sem.at[2])
    own_d.start()
    own_w.start()
    own_e.start()

    rows = lax.broadcasted_iota(jnp.int32, (128, 128), 0)
    cols = lax.broadcasted_iota(jnp.int32, (128, 128), 1)
    same = (rows < LEV) == (cols < LEV)
    distance = jnp.where(same, jnp.abs(rows - cols), 1000)
    first_half = lax.broadcasted_iota(jnp.int32, (1, 128), 1) < LEV

    def build(j, carry):
        width = jnp.where(first_half, bands_ref[2 * j] + 1, bands_ref[2 * j + 1] + 1)
        tent = jnp.maximum(width - distance, 0).astype(F32).astype(BF16)
        wide = width.astype(F32)
        scale = 1.0 / (wide * wide)
        square = jnp.dot(tent, tent, preferred_element_type=F32) * (scale * scale)
        high = square.astype(BF16)
        tents[j] = tent
        sq_hi[j] = high
        sq_lo[j] = (square - high.astype(F32)).astype(BF16)
        inv2[j] = jnp.broadcast_to(scale, (8, 128))
        return carry

    lax.fori_loop(0, PAIRS, build, 0)

    edges = (lat == 0).astype(jnp.int32) + (lat == lat_n - 1).astype(jnp.int32)
    others = sum(count - 1 for _, count, _, _, _, _ in stages)
    pl.semaphore_wait(barrier, others + 8 - 3 * edges)

    def cut(delta, size, width, before):
        if delta == 0:
            return slice(0, size), slice(before, before + size)
        if delta == 1:
            return slice(size - width, size), slice(before - width, before)
        return slice(0, width), slice(before + size, before + size + width)

    def input_copies(which, dlat, dlon):
        src_cols, dst_cols = cut(dlon, 8, 3, 3)
        src_rows, dst_rows = cut(dlat, 16, 8, 8)
        number = DIRECTIONS.index((dlat, dlon))
        pairs = ((innov_hbm, dext), (wobs_hbm, wext))
        src, dst = pairs[which]
        return pltpu.make_async_remote_copy(
            src_ref=src.at[src_cols, src_rows],
            dst_ref=dst.at[dst_cols, dst_rows],
            send_sem=in_send.at[which, number],
            recv_sem=in_recv.at[which, number],
            device_id=neighbour(dlat, dlon),
            device_id_type=MESH,
        )

    def param_copy(dlat):
        return pltpu.make_async_remote_copy(
            src_ref=params.at[1],
            dst_ref=params.at[1 - dlat],
            send_sem=par_send.at[(dlat + 1) // 2],
            recv_sem=par_recv.at[(dlat + 1) // 2],
            device_id=neighbour(dlat, 0),
            device_id_type=MESH,
        )

    def z_copy(phase, dlat, dlon):
        src_cols, dst_cols = cut(dlon, 4, 3, 3)
        src_rows, dst_rows = cut(dlat, 8, 8, 8)
        number = DIRECTIONS.index((dlat, dlon))
        src_cols = slice(src_cols.start + 3, src_cols.stop + 3)
        src_rows = slice(src_rows.start + 8, src_rows.stop + 8)
        return pltpu.make_async_remote_copy(
            src_ref=zext.at[phase, src_cols, src_rows],
            dst_ref=zext.at[phase, dst_cols, dst_rows],
            send_sem=z_send.at[phase, number],
            recv_sem=z_recv.at[phase, number],
            device_id=neighbour(dlat, dlon),
            device_id_type=MESH,
        )

    for dlat, dlon in DIRECTIONS:

        def send(dlat=dlat, dlon=dlon):
            input_copies(0, dlat, dlon).start()
            input_copies(1, dlat, dlon).start()
            if dlon == 0:
                param_copy(dlat).start()

        inside(dlat, send)

    own_d.wait()
    own_w.wait()
    own_e.wait()
    for dlat, dlon in DIRECTIONS:

        def receive(dlat=dlat, dlon=dlon):
            input_copies(0, dlat, dlon).wait_recv()
            input_copies(1, dlat, dlon).wait_recv()
            if dlon == 0:
                param_copy(dlat).wait_recv()

        inside(-dlat, receive)

    row = lax.broadcasted_iota(jnp.int32, (16, 128), 0)
    lane = lax.broadcasted_iota(jnp.int32, (16, 128), 1)
    for parity in range(2):
        fine = 2 * row - 4 + parity
        picked = []
        for kind in range(2):
            total = jnp.zeros((16, 128), F32)
            for source in range(3):
                line = jnp.broadcast_to(params[source, kind : kind + 1, :], (16, 128))
                total = total + jnp.where(lane == fine + 16 - 16 * source, line, 0.0)
            picked.append(
                jnp.broadcast_to(jnp.sum(total, axis=1, keepdims=True), (16, 128))
            )
        upper, offset = picked
        for k in range(5):
            coef[parity, k] = jnp.where(offset == float(k), 1.0 - upper, 0.0) + jnp.where(
                offset == float(k - 1), upper, 0.0
            )

    def restrict(fields):
        for parity in range(2):
            odd, even = fields(parity)
            total = jnp.zeros((4, 16, 128), F32)
            for t in range(4):
                total = total + ODD_TAPS[t] * odd[3 - t : 7 - t] + EVEN_TAPS[t] * even[3 - t : 7 - t]
            gbuf[parity] = total
        result = jnp.zeros((4, 8, 128), F32)
        for parity in range(2):
            for k in range(5):
                result = result + (
                    coef[parity, k, 4 - k : 12 - k, :][None] * gbuf[parity, :, 4 - k : 12 - k, :]
                )
        return result

    def start_field(parity):
        found = []
        for kind in range(2):
            column = []
            for b in range(7):
                at = pl.ds(4 + parity, 16, stride=2)
                weight = wext[2 * b + kind, at, :]
                wsplit[parity, kind, b] = weight
                column.append(weight * dext[2 * b + kind, at, :])
            found.append(jnp.stack(column))
        return found

    def fine_field(phase):
        def field(parity):
            along = jnp.zeros((10, 16, 128), F32)
            for k in range(5):
                along = along + coef[parity, k][None] * zext[phase, :, 4 + k : 20 + k, :]
            found = []
            for kind, taps in enumerate((ODD_TAPS, EVEN_TAPS)):
                total = taps[0] * along[0:7]
                for t in range(1, 4):
                    total = total + taps[t] * along[t : t + 7]
                found.append(wsplit[parity, kind] * total)
            return found

        return field

    first_lanes = lax.broadcasted_iota(jnp.int32, (4, 8, 128), 2) < LEV

    def split_pair(j, y):
        at = pl.multiple_of(j * 256, 256)
        e0 = ens[:, :, pl.ds(at, 128)].astype(F32)
        e1 = ens[:, :, pl.ds(at + 128, 128)].astype(F32)
        p0, p1 = e0 * y, e1 * y
        kept = jnp.where(first_lanes, p0, p1)
        moved = jnp.where(first_lanes, p1, p0)
        total = (kept + pltpu.roll(moved, LEV, 2)).reshape(32, 128)
        high = total.astype(BF16)
        low = (total - high.astype(F32)).astype(BF16)
        return e0, e1, high, low

    def combine_spread(y):
        def body(step, acc):
            for extra in range(UNROLL):
                j = step * UNROLL + extra
                e0, e1, high, low = split_pair(j, y)
                both = jnp.concatenate([high, low], axis=0)
                main = jnp.dot(both, sq_hi[j], preferred_element_type=F32)
                rest = jnp.dot(high, sq_lo[j], preferred_element_type=F32)
                out = (main[:32] + (main[32:] + rest)).reshape(4, 8, 128)
                turned = pltpu.roll(out, LEV, 2)
                acc = acc + e0 * jnp.where(first_lanes, out, turned)
                acc = acc + e1 * jnp.where(first_lanes, turned, out)
            return acc

        return lax.fori_loop(0, PAIRS // UNROLL, body, jnp.zeros((4, 8, 128), F32))

    def spread(which):
        y = yv[which]

        def body(step, carry):
            for extra in range(UNROLL):
                j = step * UNROLL + extra
                _, _, high, low = split_pair(j, y)
                both = jnp.concatenate([high, low], axis=0)
                main = jnp.dot(both, tents[j], preferred_element_type=F32)
                out = (main[:32] + main[32:]).reshape(4, 8, 128) * inv2[j][None]
                uvec[which, :, :, pl.ds(pl.multiple_of(j * 128, 128), 128)] = out
            return carry

        lax.fori_loop(0, PAIRS // UNROLL, body, 0)

    yv[0] = restrict(start_field)

    for phase in range(2):
        z = combine_spread(yv[phase])
        zext[phase, 3:7, 8:16, :] = z
        for dlat, dlon in DIRECTIONS:

            def send(dlat=dlat, dlon=dlon, phase=phase):
                z_copy(phase, dlat, dlon).start()

            inside(dlat, send)
        spread(phase)
        for dlat, dlon in DIRECTIONS:

            def receive(dlat=dlat, dlon=dlon, phase=phase):
                z_copy(phase, dlat, dlon).wait_recv()

            inside(-dlat, receive)
        yv[phase + 1] = restrict(fine_field(phase))

    z0, z1 = zext[0, 3:7, 8:16, :], zext[1, 3:7, 8:16, :]
    y0, y1, y2 = yv[0], yv[1], yv[2]
    lane1 = lax.broadcasted_iota(jnp.int32, (1, 128), 1)
    local = jnp.zeros((1, 128), F32)
    for number, (left, right) in enumerate(
        ((z0, y0), (z0, y1), (z1, y1), (z0, y2), (z1, y2))
    ):
        plane = jnp.sum(left * right, axis=0)
        value = jnp.sum(jnp.sum(plane, axis=0, keepdims=True), axis=1, keepdims=True)
        local = local + jnp.where(lane1 == number, jnp.broadcast_to(value, (1, 128)), 0.0)

    for number, (me, count, device, slots, send_sems, recv_sems) in enumerate(stages):

        def stage_copy(target, slot):
            return pltpu.make_async_remote_copy(
                src_ref=slots.at[me],
                dst_ref=slots.at[slot],
                send_sem=send_sems.at[target],
                recv_sem=recv_sems.at[slot],
                device_id=device(target),
                device_id_type=MESH,
            )

        slots[me] = local
        for step in range(1, count):
            stage_copy(lax.rem(me + step, count), me).start()
        if number == 0:
            spread(2)
        for step in range(1, count):
            other = lax.rem(me + step, count)
            stage_copy(other, other).wait_recv()
        local = slots[0]
        for slot in range(1, count):
            local = local + slots[slot]

    def picked(number):
        one = jnp.sum(jnp.where(lane1 == number, local, 0.0), axis=1, keepdims=True)
        return jnp.broadcast_to(one, (8, 128))

    a, b, d, e, f = (picked(number) for number in range(5))
    beta0 = jnp.sqrt(a / entries + EPSILON)
    alpha0 = (a + b) / (entries * beta0 * beta0)
    rest = 1.0 - alpha0
    square = (rest * rest * a + 2.0 * rest * b + d) / (beta0 * beta0)
    beta1 = jnp.sqrt(square / entries + EPSILON)
    mixed = (rest * rest * b + rest * (d + e) + f) / (beta0 * beta0)
    alpha1 = (square + mixed) / (entries * beta1 * beta1)
    back = ((rest * a + b) + (rest * b + e)) / (entries * beta0 * beta0 * beta1)
    scale = 1.0 / (beta0 * beta1)
    q2 = scale
    q1 = (1.0 + rest - alpha1) * scale
    q0 = (rest - alpha1 * rest) * scale - back / beta0
    top = lax.broadcasted_iota(jnp.int32, (8, 128), 0) == 0
    left = lax.broadcasted_iota(jnp.int32, (8, 128), 1) == 0
    table = jnp.where(top, jnp.where(left, alpha0, alpha1), jnp.where(left, beta0, beta1))
    coef_out[...] = table[0:2, 0:2]

    def finish(step, carry):
        at = pl.ds(pl.multiple_of(step * 512, 512), 512)

        def wide(q):
            return jnp.concatenate([q] * 4, axis=1)[None]

        vec_out[:, :, at] = (
            wide(q0) * uvec[0, :, :, at] + wide(q1) * uvec[1, :, :, at] + wide(q2) * uvec[2, :, :, at]
        ).astype(BF16)
        return carry

    lax.fori_loop(0, M * LEV // 512, finish, 0)

    for dlat, dlon in DIRECTIONS:

        def drain(dlat=dlat, dlon=dlon):
            input_copies(0, dlat, dlon).wait_send()
            input_copies(1, dlat, dlon).wait_send()
            z_copy(0, dlat, dlon).wait_send()
            z_copy(1, dlat, dlon).wait_send()
            if dlon == 0:
                param_copy(dlat).wait_send()

        inside(dlat, drain)
    for me, count, device, slots, send_sems, recv_sems in stages:
        for step in range(1, count):
            target = lax.rem(me + step, count)
            pltpu.make_async_remote_copy(
                src_ref=slots.at[me],
                dst_ref=slots.at[me],
                send_sem=send_sems.at[target],
                recv_sem=recv_sems.at[me],
                device_id=device(target),
                device_id_type=MESH,
            ).wait_send()


def per_device(topo, ensemble, innovation, obs_weight, lat_offset, lat_weight, band_widths):
    zh_n, x_n, zl_n, y_n, core_n = topo
    entries = float(4 * 8 * M * LEV * zh_n * x_n * zl_n * y_n * core_n)
    vmem = pltpu.VMEM
    dma = pltpu.SemaphoreType.DMA
    group_a, group_b, group_c = x_n * core_n, y_n, zh_n * zl_n
    anywhere = pl.BlockSpec(memory_space=pl.ANY)
    in_vmem = pl.BlockSpec(memory_space=pltpu.VMEM)
    return pl.pallas_call(
        functools.partial(kernel, topo, entries),
        out_shape=(
            jax.ShapeDtypeStruct((2, 2), F32),
            jax.ShapeDtypeStruct((4, 8, M * LEV), BF16),
        ),
        in_specs=[
            anywhere,
            anywhere,
            anywhere,
            in_vmem,
            in_vmem,
            pl.BlockSpec(memory_space=pltpu.SMEM),
        ],
        out_specs=(in_vmem, in_vmem),
        scratch_shapes=[
            vmem((4, 8, 2 * M * LEV), BF16),
            vmem((14, 40, 128), F32),
            vmem((14, 40, 128), F32),
            vmem((2, 2, 7, 16, 128), F32),
            vmem((2, 10, 24, 128), F32),
            vmem((3, 4, 8, 128), F32),
            vmem((3, 8, 128), F32),
            vmem((2, 5, 16, 128), F32),
            vmem((2, 4, 16, 128), F32),
            vmem((PAIRS, 128, 128), BF16),
            vmem((PAIRS, 128, 128), BF16),
            vmem((PAIRS, 128, 128), BF16),
            vmem((PAIRS, 8, 128), F32),
            vmem((3, 4, 8, M * LEV), F32),
            vmem((group_a, 1, 128), F32),
            vmem((group_b, 1, 128), F32),
            vmem((group_c, 1, 128), F32),
            dma((3,)),
            dma((2, 8)),
            dma((2, 8)),
            dma((2,)),
            dma((2,)),
            dma((2, 8)),
            dma((2, 8)),
            dma((group_a,)),
            dma((group_a,)),
            dma((group_b,)),
            dma((group_b,)),
            dma((group_c,)),
            dma((group_c,)),
        ],
        compiler_params=pltpu.CompilerParams(
            collective_id=0, has_side_effects=True, vmem_limit_bytes=32 * 1024 * 1024
        ),
        name="lanczos",
    )(
        ensemble,
        innovation,
        obs_weight,
        lat_offset.reshape(1, 16),
        lat_weight.reshape(1, 16),
        band_widths,
    )


def solution(mesh):
    return jax.shard_map(
        functools.partial(per_device, TOPO),
        mesh=mesh,
        in_specs=(
            P("lon", "lat", None),
            P("lon", "lat", None),
            P("lon", "lat", None),
            P("lat"),
            P("lat"),
            P(),
        ),
        out_specs=(P(), P("lon", "lat", None)),
        check_vma=False,
    )
```

```python
import functools

import jax
import jax.numpy as jnp
from jax import lax
from jax.experimental import pallas as pl
from jax.experimental.pallas import tpu as pltpu
from jax.sharding import PartitionSpec as P

M = 80
LEV = 64
PAIRS = M // 2
EVEN_TAPS = (-0.0234375, 0.2265625, 0.8671875, -0.0703125)
ODD_TAPS = (-0.0703125, 0.8671875, 0.2265625, -0.0234375)
EPSILON = 1e-06
F32 = jnp.float32
BF16 = jnp.bfloat16
MESH = pl.DeviceIdType.MESH
TOPO = (4, 4, 3, 8, 2)
DIRECTIONS = ((1, 1), (1, -1), (-1, 1), (-1, -1), (1, 0), (-1, 0), (0, 1), (0, -1))
UNROLL = 8


def kernel(
    topo,
    entries,
    ens_hbm,
    innov_hbm,
    wobs_hbm,
    offset_hbm,
    weight_hbm,
    bands_hbm,
    table_out,
    u_hbm,
    offset_ref,
    weight_ref,
    bands_ref,
    ens,
    down,
    fext,
    wext,
    wsplit,
    zext,
    yv,
    params,
    coef,
    gbuf,
    tents,
    sq_hi,
    sq_lo,
    inv2,
    uvec,
    red_a,
    red_b,
    red_c,
    local_sem,
    in_send,
    in_recv,
    par_send,
    par_recv,
    z_send,
    z_recv,
    a_send,
    a_recv,
    b_send,
    b_recv,
    c_send,
    c_recv,
):
    zh_n, x_n, zl_n, y_n, core_n = topo
    lat_n, lon_n = zh_n * x_n, zl_n * y_n * core_n
    lat, lon = lax.axis_index("lat"), lax.axis_index("lon")
    z_hi, x = lat // x_n, lat % x_n
    z_lo, y_core = lon // (y_n * core_n), lon % (y_n * core_n)
    y_pos, core = y_core // core_n, y_core % core_n

    def neighbour(dlat, dlon):
        return (lat + dlat, lax.rem(lon + dlon + lon_n, lon_n))

    def inside(dlat, body):
        if dlat == 0:
            body()
        else:
            pl.when((lat + dlat >= 0) & (lat + dlat < lat_n))(body)

    def dev_a(i):
        return (z_hi * x_n + i // core_n, lon - core + i % core_n)

    def dev_b(i):
        return (lat, z_lo * (y_n * core_n) + i * core_n + core)

    def dev_c(i):
        return ((i // zl_n) * x_n + x, (i % zl_n) * (y_n * core_n) + y_core)

    stages = (
        (x * core_n + core, x_n * core_n, dev_a, red_a, a_send, a_recv),
        (y_pos, y_n, dev_b, red_b, b_send, b_recv),
        (z_hi * zl_n + z_lo, zh_n * zl_n, dev_c, red_c, c_send, c_recv),
    )

    small = [
        pltpu.make_async_copy(src, dst, local_sem.at[3 + number])
        for number, (src, dst) in enumerate(
            ((bands_hbm, bands_ref), (weight_hbm, weight_ref), (offset_hbm, offset_ref))
        )
    ]
    for copy in small:
        copy.start()
    own_d = pltpu.make_async_copy(innov_hbm, down, local_sem.at[0])
    own_w = pltpu.make_async_copy(wobs_hbm, wext.at[3:11, 8:24], local_sem.at[1])
    own_e = pltpu.make_async_copy(ens_hbm, ens, local_sem.at[2])

    fext[...] = jnp.zeros(fext.shape, F32)
    wext[...] = jnp.zeros(wext.shape, F32)
    zext[...] = jnp.zeros(zext.shape, F32)
    params[...] = jnp.zeros(params.shape, F32)
    barrier = pltpu.get_barrier_semaphore()
    for dlat, dlon in DIRECTIONS:

        def greet(dlat=dlat, dlon=dlon):
            pl.semaphore_signal(
                barrier, inc=1, device_id=neighbour(dlat, dlon), device_id_type=MESH
            )

        inside(dlat, greet)
    for me, count, device, _, _, _ in stages:
        for step in range(1, count):
            pl.semaphore_signal(
                barrier,
                inc=1,
                device_id=device(lax.rem(me + step, count)),
                device_id_type=MESH,
            )

    own_d.start()
    own_w.start()
    own_e.start()
    for copy in small:
        copy.wait()
    params[1, 0:1, 0:16] = weight_ref[...]
    params[1, 1:2, 0:16] = offset_ref[...].astype(F32)

    rows = lax.broadcasted_iota(jnp.int32, (128, 128), 0)
    cols = lax.broadcasted_iota(jnp.int32, (128, 128), 1)
    same = (rows < LEV) == (cols < LEV)
    distance = jnp.where(same, jnp.abs(rows - cols), 1000)
    first_half = lax.broadcasted_iota(jnp.int32, (1, 128), 1) < LEV

    def build(j):
        width = jnp.where(first_half, bands_ref[0, 2 * j] + 1, bands_ref[0, 2 * j + 1] + 1)
        tent = jnp.maximum(width - distance, 0).astype(F32).astype(BF16)
        wide = width.astype(F32)
        scale = 1.0 / (wide * wide)
        square = jnp.dot(tent, tent, preferred_element_type=F32) * (scale * scale)
        high = square.astype(BF16)
        tents[j] = tent
        sq_hi[j] = high
        sq_lo[j] = (square - high.astype(F32)).astype(BF16)
        inv2[j] = jnp.broadcast_to(scale, (8, 128))

    def build_some(step, carry):
        for extra in range(UNROLL):
            build(step * UNROLL + extra)
        return carry

    lax.fori_loop(0, PAIRS // UNROLL, build_some, 0)

    own_d.wait()
    own_w.wait()
    fext[3:11, 8:24, :] = down[...] * wext[3:11, 8:24, :]
    edges = (lat == 0).astype(jnp.int32) + (lat == lat_n - 1).astype(jnp.int32)
    others = sum(count - 1 for _, count, _, _, _, _ in stages)
    pl.semaphore_wait(barrier, others + 8 - 3 * edges)

    def cut(delta, size, width, before):
        if delta == 0:
            return slice(0, size), slice(before, before + size)
        if delta == 1:
            return slice(size - width, size), slice(before - width, before)
        return slice(0, width), slice(before + size, before + size + width)

    def shifted(part, by):
        return slice(part.start + by, part.stop + by)

    def input_copy(which, dlat, dlon):
        src_cols, dst_cols = cut(dlon, 8, 3, 3)
        src_rows, dst_rows = cut(dlat, 16, 4, 8)
        number = DIRECTIONS.index((dlat, dlon))
        if which == 0:
            src, dst = fext.at[shifted(src_cols, 3), shifted(src_rows, 8)], fext
        else:
            src, dst = wobs_hbm.at[src_cols, src_rows], wext
        return pltpu.make_async_remote_copy(
            src_ref=src,
            dst_ref=dst.at[dst_cols, dst_rows],
            send_sem=in_send.at[which, number],
            recv_sem=in_recv.at[which, number],
            device_id=neighbour(dlat, dlon),
            device_id_type=MESH,
        )

    def param_copy(dlat):
        return pltpu.make_async_remote_copy(
            src_ref=params.at[1],
            dst_ref=params.at[1 - dlat],
            send_sem=par_send.at[(dlat + 1) // 2],
            recv_sem=par_recv.at[(dlat + 1) // 2],
            device_id=neighbour(dlat, 0),
            device_id_type=MESH,
        )

    def z_copy(phase, dlat, dlon):
        src_cols, dst_cols = cut(dlon, 4, 3, 3)
        src_rows, dst_rows = cut(dlat, 8, 4, 8)
        number = DIRECTIONS.index((dlat, dlon))
        return pltpu.make_async_remote_copy(
            src_ref=zext.at[phase, shifted(src_cols, 3), shifted(src_rows, 8)],
            dst_ref=zext.at[phase, dst_cols, dst_rows],
            send_sem=z_send.at[phase, number],
            recv_sem=z_recv.at[phase, number],
            device_id=neighbour(dlat, dlon),
            device_id_type=MESH,
        )

    for dlat in (-1, 1):
        inside(dlat, lambda dlat=dlat: param_copy(dlat).start())
    for which in range(2):
        for dlat, dlon in DIRECTIONS:
            inside(
                dlat,
                lambda which=which, dlat=dlat, dlon=dlon: input_copy(which, dlat, dlon).start(),
            )

    def receive_input(which):
        for dlat, dlon in DIRECTIONS:
            inside(
                -dlat,
                lambda dlat=dlat, dlon=dlon: input_copy(which, dlat, dlon).wait_recv(),
            )

    for dlat in (-1, 1):
        inside(-dlat, lambda dlat=dlat: param_copy(dlat).wait_recv())

    row = lax.broadcasted_iota(jnp.int32, (16, 128), 0)
    lane = lax.broadcasted_iota(jnp.int32, (16, 128), 1)
    for parity in range(2):
        fine = 2 * row - 4 + parity
        picked = []
        for kind in range(2):
            total = jnp.zeros((16, 128), F32)
            for source in range(3):
                line = jnp.broadcast_to(params[source, kind : kind + 1, :], (16, 128))
                total = total + jnp.where(lane == fine + 16 - 16 * source, line, 0.0)
            picked.append(
                jnp.broadcast_to(jnp.sum(total, axis=1, keepdims=True), (16, 128))
            )
        upper, offset = picked
        for k in range(5):
            coef[parity, k] = jnp.where(offset == float(k), 1.0 - upper, 0.0) + jnp.where(
                offset == float(k - 1), upper, 0.0
            )

    def restrict(fields):
        for parity in range(2):
            odd, even = fields(parity)
            total = jnp.zeros((4, 16, 128), F32)
            for t in range(4):
                total = total + ODD_TAPS[t] * odd[3 - t : 7 - t] + EVEN_TAPS[t] * even[3 - t : 7 - t]
            gbuf[parity] = total
        result = jnp.zeros((4, 8, 128), F32)
        for parity in range(2):
            for k in range(5):
                result = result + (
                    coef[parity, k, 4 - k : 12 - k, :][None] * gbuf[parity, :, 4 - k : 12 - k, :]
                )
        return result

    def split_rows(ext, parity, kind):
        at = pl.ds(4 + parity, 16, stride=2)
        return jnp.stack([ext[2 * b + kind, at, :] for b in range(7)])

    def start_field(parity):
        return [split_rows(fext, parity, kind) for kind in range(2)]

    def fine_field(phase):
        def field(parity):
            along = jnp.zeros((10, 16, 128), F32)
            for k in range(5):
                along = along + coef[parity, k][None] * zext[phase, :, 4 + k : 20 + k, :]
            found = []
            for kind, taps in enumerate((ODD_TAPS, EVEN_TAPS)):
                total = taps[0] * along[0:7]
                for t in range(1, 4):
                    total = total + taps[t] * along[t : t + 7]
                found.append(wsplit[parity, kind] * total)
            return found

        return field

    first_lanes = lax.broadcasted_iota(jnp.int32, (4, 8, 128), 2) < LEV

    def split_pair(j, y):
        at = j * 256 if isinstance(j, int) else pl.multiple_of(j * 256, 256)
        e0 = ens[:, :, pl.ds(at, 128)].astype(F32)
        e1 = ens[:, :, pl.ds(at + 128, 128)].astype(F32)
        p0, p1 = e0 * y, e1 * y
        kept = jnp.where(first_lanes, p0, p1)
        moved = jnp.where(first_lanes, p1, p0)
        total = (kept + pltpu.roll(moved, LEV, 2)).reshape(32, 128)
        high = total.astype(BF16)
        low = (total - high.astype(F32)).astype(BF16)
        return e0, e1, high, low

    def combine_spread(y):
        acc = jnp.zeros((4, 8, 128), F32)
        for j in range(PAIRS):
            e0, e1, high, low = split_pair(j, y)
            both = jnp.concatenate([high, low], axis=0)
            main = jnp.dot(both, sq_hi[j], preferred_element_type=F32)
            rest = jnp.dot(high, sq_lo[j], preferred_element_type=F32)
            out = (main[:32] + (main[32:] + rest)).reshape(4, 8, 128)
            turned = pltpu.roll(out, LEV, 2)
            acc = acc + e0 * jnp.where(first_lanes, out, turned)
            acc = acc + e1 * jnp.where(first_lanes, turned, out)
        return acc

    def spread(which):
        y = yv[which]

        def body(step, carry):
            for extra in range(UNROLL):
                j = step * UNROLL + extra
                _, _, high, low = split_pair(j, y)
                both = jnp.concatenate([high, low], axis=0)
                main = jnp.dot(both, tents[j], preferred_element_type=F32)
                out = (main[:32] + main[32:]).reshape(4, 8, 128) * inv2[j][None]
                uvec[which, :, :, pl.ds(pl.multiple_of(j * 128, 128), 128)] = out
            return carry

        lax.fori_loop(0, PAIRS // UNROLL, body, 0)

    own_e.wait()
    receive_input(0)
    yv[0] = restrict(start_field)

    for phase in range(2):
        z = combine_spread(yv[phase])
        zext[phase, 3:7, 8:16, :] = z
        for dlat, dlon in DIRECTIONS:

            def send(dlat=dlat, dlon=dlon, phase=phase):
                z_copy(phase, dlat, dlon).start()

            inside(dlat, send)
        spread(phase)
        pltpu.make_async_copy(uvec.at[phase], u_hbm.at[phase], local_sem.at[6 + phase]).start()
        if phase == 0:
            receive_input(1)
            for parity in range(2):
                for kind in range(2):
                    wsplit[parity, kind] = split_rows(wext, parity, kind)
        for dlat, dlon in DIRECTIONS:

            def receive(dlat=dlat, dlon=dlon, phase=phase):
                z_copy(phase, dlat, dlon).wait_recv()

            inside(-dlat, receive)
        yv[phase + 1] = restrict(fine_field(phase))

    lane1 = lax.broadcasted_iota(jnp.int32, (1, 128), 1)
    local = jnp.zeros((1, 128), F32)
    for number, (left, right) in enumerate(((0, 0), (0, 1), (1, 1), (0, 2), (1, 2))):
        plane = jnp.sum(zext[left, 3:7, 8:16, :] * yv[right], axis=0)
        value = jnp.sum(jnp.sum(plane, axis=0, keepdims=True), axis=1, keepdims=True)
        local = local + jnp.where(lane1 == number, jnp.broadcast_to(value, (1, 128)), 0.0)

    for number, (me, count, device, slots, send_sems, recv_sems) in enumerate(stages):

        def stage_copy(target, slot):
            return pltpu.make_async_remote_copy(
                src_ref=slots.at[me],
                dst_ref=slots.at[slot],
                send_sem=send_sems.at[target],
                recv_sem=recv_sems.at[slot],
                device_id=device(target),
                device_id_type=MESH,
            )

        slots[me] = local
        for step in range(1, count):
            stage_copy(lax.rem(me + step, count), me).start()
        if number == 0:
            spread(2)
            pltpu.make_async_copy(uvec.at[2], u_hbm.at[2], local_sem.at[8]).start()
        for step in range(1, count):
            other = lax.rem(me + step, count)
            stage_copy(other, other).wait_recv()
        local = slots[0]
        for slot in range(1, count):
            local = local + slots[slot]

    def picked(number):
        one = jnp.sum(jnp.where(lane1 == number, local, 0.0), axis=1, keepdims=True)
        return jnp.broadcast_to(one, (8, 128))

    a, b, d, e, f = (picked(number) for number in range(5))
    beta0 = jnp.sqrt(a / entries + EPSILON)
    alpha0 = (a + b) / (entries * beta0 * beta0)
    rest = 1.0 - alpha0
    square = (rest * rest * a + 2.0 * rest * b + d) / (beta0 * beta0)
    beta1 = jnp.sqrt(square / entries + EPSILON)
    mixed = (rest * rest * b + rest * (d + e) + f) / (beta0 * beta0)
    alpha1 = (square + mixed) / (entries * beta1 * beta1)
    back = ((rest * a + b) + (rest * b + e)) / (entries * beta0 * beta0 * beta1)
    scale = 1.0 / (beta0 * beta1)
    q2 = scale
    q1 = (1.0 + rest - alpha1) * scale
    q0 = (rest - alpha1 * rest) * scale - back / beta0
    row8 = lax.broadcasted_iota(jnp.int32, (8, 128), 0)
    left = lax.broadcasted_iota(jnp.int32, (8, 128), 1) == 0
    table = jnp.where(row8 == 0, jnp.where(left, alpha0, alpha1), jnp.where(left, beta0, beta1))
    for number, q in enumerate((q0, q1, q2)):
        table = jnp.where(row8 == 2 + number, q, table)
    table_out[...] = table

    for number in range(3):
        pltpu.make_async_copy(uvec.at[number], u_hbm.at[number], local_sem.at[6 + number]).wait()
    for dlat in (-1, 1):
        inside(dlat, lambda dlat=dlat: param_copy(dlat).wait_send())
    for dlat, dlon in DIRECTIONS:

        def drain(dlat=dlat, dlon=dlon):
            for which in range(2):
                input_copy(which, dlat, dlon).wait_send()
                z_copy(which, dlat, dlon).wait_send()

        inside(dlat, drain)
    for me, count, device, slots, send_sems, recv_sems in stages:
        for step in range(1, count):
            target = lax.rem(me + step, count)
            pltpu.make_async_remote_copy(
                src_ref=slots.at[me],
                dst_ref=slots.at[me],
                send_sem=send_sems.at[target],
                recv_sem=recv_sems.at[me],
                device_id=device(target),
                device_id_type=MESH,
            ).wait_send()


def finish(table_hbm, u_hbm, coef_hbm, vec_hbm, table, corner, u, vec, sems):
    head = pltpu.make_async_copy(table_hbm, table, sems.at[0, 4])
    tail = pltpu.make_async_copy(corner, coef_hbm, sems.at[1, 4])
    loads = [pltpu.make_async_copy(u_hbm.at[:, c], u.at[:, c], sems.at[0, c]) for c in range(4)]
    stores = [pltpu.make_async_copy(vec.at[c], vec_hbm.at[c], sems.at[1, c]) for c in range(4)]
    head.start()
    for load in loads:
        load.start()
    head.wait()
    corner[...] = table[0:2, 0:2]
    tail.start()
    q = [jnp.broadcast_to(table[2 + k : 3 + k, :], (8, 128)) for k in range(3)]
    wide = [jnp.concatenate([part] * 8, axis=1) for part in q]
    for c in range(4):
        loads[c].wait()
        for step in range(M * LEV // 1024):
            at = slice(step * 1024, (step + 1) * 1024)
            vec[c, :, at] = (
                wide[0] * u[0, c, :, at] + wide[1] * u[1, c, :, at] + wide[2] * u[2, c, :, at]
            ).astype(BF16)
        stores[c].start()
    for store in stores:
        store.wait()
    tail.wait()


def per_device(topo, ensemble, innovation, obs_weight, lat_offset, lat_weight, band_widths):
    zh_n, x_n, zl_n, y_n, core_n = topo
    entries = float(4 * 8 * M * LEV * zh_n * x_n * zl_n * y_n * core_n)
    vmem = pltpu.VMEM
    dma = pltpu.SemaphoreType.DMA
    group_a, group_b, group_c = x_n * core_n, y_n, zh_n * zl_n
    anywhere = pl.BlockSpec(memory_space=pl.ANY)
    in_vmem = pl.BlockSpec(memory_space=pltpu.VMEM)
    table, u = pl.pallas_call(
        functools.partial(kernel, topo, entries),
        out_shape=(
            jax.ShapeDtypeStruct((8, 128), F32),
            jax.ShapeDtypeStruct((3, 4, 8, M * LEV), F32),
        ),
        in_specs=[
            anywhere,
            anywhere,
            anywhere,
            anywhere,
            anywhere,
            anywhere,
        ],
        out_specs=(in_vmem, anywhere),
        scratch_shapes=[
            vmem((1, 16), jnp.int32),
            vmem((1, 16), F32),
            pltpu.SMEM((1, M), jnp.int32),
            vmem((4, 8, 2 * M * LEV), BF16),
            vmem((8, 16, 128), F32),
            vmem((14, 40, 128), F32),
            vmem((14, 40, 128), F32),
            vmem((2, 2, 7, 16, 128), F32),
            vmem((2, 10, 24, 128), F32),
            vmem((3, 4, 8, 128), F32),
            vmem((3, 8, 128), F32),
            vmem((2, 5, 16, 128), F32),
            vmem((2, 4, 16, 128), F32),
            vmem((PAIRS, 128, 128), BF16),
            vmem((PAIRS, 128, 128), BF16),
            vmem((PAIRS, 128, 128), BF16),
            vmem((PAIRS, 8, 128), F32),
            vmem((3, 4, 8, M * LEV), F32),
            vmem((group_a, 1, 128), F32),
            vmem((group_b, 1, 128), F32),
            vmem((group_c, 1, 128), F32),
            dma((9,)),
            dma((2, 8)),
            dma((2, 8)),
            dma((2,)),
            dma((2,)),
            dma((2, 8)),
            dma((2, 8)),
            dma((group_a,)),
            dma((group_a,)),
            dma((group_b,)),
            dma((group_b,)),
            dma((group_c,)),
            dma((group_c,)),
        ],
        compiler_params=pltpu.CompilerParams(
            collective_id=0, has_side_effects=True, vmem_limit_bytes=62 * 1024 * 1024
        ),
        name="lanczos",
    )(
        ensemble,
        innovation,
        obs_weight,
        lat_offset.reshape(1, 16),
        lat_weight.reshape(1, 16),
        band_widths.reshape(1, M),
    )
    return pl.pallas_call(
        finish,
        out_shape=(
            jax.ShapeDtypeStruct((2, 2), F32),
            jax.ShapeDtypeStruct((4, 8, M * LEV), BF16),
        ),
        in_specs=[anywhere, anywhere],
        out_specs=(anywhere, anywhere),
        scratch_shapes=[
            vmem((8, 128), F32),
            vmem((2, 2), F32),
            vmem((3, 4, 8, M * LEV), F32),
            vmem((4, 8, M * LEV), BF16),
            dma((2, 5)),
        ],
        compiler_params=pltpu.CompilerParams(vmem_limit_bytes=62 * 1024 * 1024),
        name="finish",
    )(table, u)


def solution(mesh):
    return jax.shard_map(
        functools.partial(per_device, TOPO),
        mesh=mesh,
        in_specs=(
            P("lon", "lat", None),
            P("lon", "lat", None),
            P("lon", "lat", None),
            P("lat"),
            P("lat"),
            P(),
        ),
        out_specs=(P(), P("lon", "lat", None)),
        check_vma=False,
    )
```

```python
import functools

import jax
import jax.numpy as jnp
from jax import lax
from jax.experimental import pallas as pl
from jax.experimental.pallas import tpu as pltpu
from jax.sharding import PartitionSpec as P

M = 80
LEV = 64
PAIRS = M // 2
EVEN_TAPS = (-0.0234375, 0.2265625, 0.8671875, -0.0703125)
ODD_TAPS = (-0.0703125, 0.8671875, 0.2265625, -0.0234375)
EPSILON = 1e-06
F32 = jnp.float32
BF16 = jnp.bfloat16
MESH = pl.DeviceIdType.MESH
TOPO = (4, 4, 3, 8, 2)
DIRECTIONS = ((1, 1), (1, -1), (-1, 1), (-1, -1), (1, 0), (-1, 0), (0, 1), (0, -1))
UNROLL = 8


def kernel(
    topo,
    entries,
    ens_hbm,
    innov_hbm,
    wobs_hbm,
    offset_hbm,
    weight_hbm,
    bands_hbm,
    table_out,
    uvec,
    offset_ref,
    weight_ref,
    bands_ref,
    ens,
    down,
    fown,
    hbuf,
    ybuf,
    yin,
    wext,
    wsplit,
    zext,
    yv,
    params,
    coef,
    gbuf,
    tents,
    sq_hi,
    sq_lo,
    inv2,
    red_a,
    red_b,
    red_c,
    local_sem,
    in_send,
    in_recv,
    par_send,
    par_recv,
    z_send,
    z_recv,
    a_send,
    a_recv,
    b_send,
    b_recv,
    c_send,
    c_recv,
):
    zh_n, x_n, zl_n, y_n, core_n = topo
    lat_n, lon_n = zh_n * x_n, zl_n * y_n * core_n
    lat, lon = lax.axis_index("lat"), lax.axis_index("lon")
    z_hi, x = lat // x_n, lat % x_n
    z_lo, y_core = lon // (y_n * core_n), lon % (y_n * core_n)
    y_pos, core = y_core // core_n, y_core % core_n

    def neighbour(dlat, dlon):
        return (lat + dlat, lax.rem(lon + dlon + lon_n, lon_n))

    def inside(dlat, body):
        if dlat == 0:
            body()
        else:
            pl.when((lat + dlat >= 0) & (lat + dlat < lat_n))(body)

    def dev_a(i):
        return (z_hi * x_n + i // core_n, lon - core + i % core_n)

    def dev_b(i):
        return (lat, z_lo * (y_n * core_n) + i * core_n + core)

    def dev_c(i):
        return ((i // zl_n) * x_n + x, (i % zl_n) * (y_n * core_n) + y_core)

    stages = (
        (x * core_n + core, x_n * core_n, dev_a, red_a, a_send, a_recv),
        (y_pos, y_n, dev_b, red_b, b_send, b_recv),
        (z_hi * zl_n + z_lo, zh_n * zl_n, dev_c, red_c, c_send, c_recv),
    )

    small = [
        pltpu.make_async_copy(src, dst, local_sem.at[3 + number])
        for number, (src, dst) in enumerate(
            ((bands_hbm, bands_ref), (weight_hbm, weight_ref), (offset_hbm, offset_ref))
        )
    ]
    for copy in small:
        copy.start()
    own_d = pltpu.make_async_copy(innov_hbm, down, local_sem.at[0])
    own_w = pltpu.make_async_copy(wobs_hbm, wext.at[3:11, 8:24], local_sem.at[1])
    own_e = pltpu.make_async_copy(ens_hbm, ens, local_sem.at[2])

    fown[...] = jnp.zeros(fown.shape, F32)
    hbuf[...] = jnp.zeros(hbuf.shape, F32)
    yin[...] = jnp.zeros(yin.shape, F32)
    wext[...] = jnp.zeros(wext.shape, F32)
    zext[...] = jnp.zeros(zext.shape, F32)
    params[...] = jnp.zeros(params.shape, F32)
    barrier = pltpu.get_barrier_semaphore()
    for dlat, dlon in DIRECTIONS:

        def greet(dlat=dlat, dlon=dlon):
            pl.semaphore_signal(
                barrier, inc=1, device_id=neighbour(dlat, dlon), device_id_type=MESH
            )

        inside(dlat, greet)
    for me, count, device, _, _, _ in stages:
        for step in range(1, count):
            pl.semaphore_signal(
                barrier,
                inc=1,
                device_id=device(lax.rem(me + step, count)),
                device_id_type=MESH,
            )

    own_d.start()
    own_w.start()
    own_e.start()
    for copy in small:
        copy.wait()
    params[1, 0:1, 0:16] = weight_ref[...]
    params[1, 1:2, 0:16] = offset_ref[...].astype(F32)

    rows = lax.broadcasted_iota(jnp.int32, (128, 128), 0)
    cols = lax.broadcasted_iota(jnp.int32, (128, 128), 1)
    same = (rows < LEV) == (cols < LEV)
    distance = jnp.where(same, jnp.abs(rows - cols), 1000)
    first_half = lax.broadcasted_iota(jnp.int32, (1, 128), 1) < LEV

    def build(j):
        width = jnp.where(first_half, bands_ref[0, 2 * j] + 1, bands_ref[0, 2 * j + 1] + 1)
        tent = jnp.maximum(width - distance, 0).astype(F32).astype(BF16)
        wide = width.astype(F32)
        scale = 1.0 / (wide * wide)
        square = jnp.dot(tent, tent, preferred_element_type=F32) * (scale * scale)
        high = square.astype(BF16)
        tents[j] = tent
        sq_hi[j] = high
        sq_lo[j] = (square - high.astype(F32)).astype(BF16)
        inv2[j] = jnp.broadcast_to(scale, (8, 128))

    def build_some(step, carry):
        for extra in range(UNROLL):
            build(step * UNROLL + extra)
        return carry

    lax.fori_loop(0, PAIRS // UNROLL, build_some, 0)

    own_d.wait()
    own_w.wait()
    fown[:, 8:24, :] = down[...] * wext[3:11, 8:24, :]

    row = lax.broadcasted_iota(jnp.int32, (16, 128), 0)
    lane = lax.broadcasted_iota(jnp.int32, (16, 128), 1)

    def find_coef(sources):
        for parity in range(2):
            fine = 2 * row - 4 + parity
            picked = []
            for kind in range(2):
                total = jnp.zeros((16, 128), F32)
                for source in sources:
                    line = jnp.broadcast_to(params[source, kind : kind + 1, :], (16, 128))
                    total = total + jnp.where(lane == fine + 16 - 16 * source, line, 0.0)
                picked.append(
                    jnp.broadcast_to(jnp.sum(total, axis=1, keepdims=True), (16, 128))
                )
            upper, offset = picked
            for k in range(5):
                coef[parity, k] = jnp.where(offset == float(k), 1.0 - upper, 0.0) + jnp.where(
                    offset == float(k - 1), upper, 0.0
                )

    find_coef((1,))
    shares = [jnp.zeros((8, 16, 128), F32) for _ in range(5)]
    for parity in range(2):
        at = pl.ds(4 + parity, 16, stride=2)
        columns = [jnp.zeros((16, 128), F32) for _ in range(8)]
        for c in range(4):
            even, odd = fown[2 * c, at, :], fown[2 * c + 1, at, :]
            for t in range(4):
                columns[c + t] = columns[c + t] + EVEN_TAPS[t] * even
                columns[c + 1 + t] = columns[c + 1 + t] + ODD_TAPS[t] * odd
        along = jnp.stack(columns)
        shares = [shares[k] + coef[parity, k][None] * along for k in range(5)]
    for k in range(5):
        hbuf[k, :, 8:24, :] = shares[k]
    total = jnp.zeros((8, 24, 128), F32)
    for k in range(5):
        total = total + hbuf[k, :, 4 - k : 28 - k, :]
    ybuf[...] = total

    edges = (lat == 0).astype(jnp.int32) + (lat == lat_n - 1).astype(jnp.int32)
    others = sum(count - 1 for _, count, _, _, _, _ in stages)
    pl.semaphore_wait(barrier, others + 8 - 3 * edges)

    def cut(delta, size, width, before):
        if delta == 0:
            return slice(0, size), slice(before, before + size)
        if delta == 1:
            return slice(size - width, size), slice(before - width, before)
        return slice(0, width), slice(before + size, before + size + width)

    def shifted(part, by):
        return slice(part.start + by, part.stop + by)

    def weight_copy(dlat, dlon):
        src_cols, dst_cols = cut(dlon, 8, 3, 3)
        src_rows, dst_rows = cut(dlat, 16, 4, 8)
        number = DIRECTIONS.index((dlat, dlon))
        return pltpu.make_async_remote_copy(
            src_ref=wobs_hbm.at[src_cols, src_rows],
            dst_ref=wext.at[dst_cols, dst_rows],
            send_sem=in_send.at[1, number],
            recv_sem=in_recv.at[1, number],
            device_id=neighbour(dlat, dlon),
            device_id_type=MESH,
        )

    def share_copy(dlat, dlon):
        number = DIRECTIONS.index((dlat, dlon))
        src_cols, dst_cols = (
            (slice(2, 6), slice(0, 4)),
            (slice(6, 8), slice(0, 2)),
            (slice(0, 2), slice(2, 4)),
        )[dlon]
        src_rows, dst_rows = (
            (slice(8, 16), slice(0, 8)),
            (slice(16, 18), slice(0, 2)),
            (slice(6, 8), slice(6, 8)),
        )[dlat]
        return pltpu.make_async_remote_copy(
            src_ref=ybuf.at[src_cols, src_rows],
            dst_ref=yin.at[number, dst_cols, dst_rows],
            send_sem=in_send.at[0, number],
            recv_sem=in_recv.at[0, number],
            device_id=neighbour(dlat, dlon),
            device_id_type=MESH,
        )

    def param_copy(dlat):
        return pltpu.make_async_remote_copy(
            src_ref=params.at[1],
            dst_ref=params.at[1 - dlat],
            send_sem=par_send.at[(dlat + 1) // 2],
            recv_sem=par_recv.at[(dlat + 1) // 2],
            device_id=neighbour(dlat, 0),
            device_id_type=MESH,
        )

    def z_copy(phase, dlat, dlon):
        src_cols, dst_cols = cut(dlon, 4, 3, 3)
        src_rows, dst_rows = cut(dlat, 8, 4, 8)
        number = DIRECTIONS.index((dlat, dlon))
        return pltpu.make_async_remote_copy(
            src_ref=zext.at[phase, shifted(src_cols, 3), shifted(src_rows, 8)],
            dst_ref=zext.at[phase, dst_cols, dst_rows],
            send_sem=z_send.at[phase, number],
            recv_sem=z_recv.at[phase, number],
            device_id=neighbour(dlat, dlon),
            device_id_type=MESH,
        )

    for dlat, dlon in DIRECTIONS:
        inside(dlat, lambda dlat=dlat, dlon=dlon: share_copy(dlat, dlon).start())
    for dlat in (-1, 1):
        inside(dlat, lambda dlat=dlat: param_copy(dlat).start())
    for dlat, dlon in DIRECTIONS:
        inside(dlat, lambda dlat=dlat, dlon=dlon: weight_copy(dlat, dlon).start())

    def restrict(fields):
        shares = [jnp.zeros((4, 16, 128), F32) for _ in range(5)]
        for parity in range(2):
            odd, even = fields(parity)
            total = jnp.zeros((4, 16, 128), F32)
            for t in range(4):
                total = total + ODD_TAPS[t] * odd[3 - t : 7 - t] + EVEN_TAPS[t] * even[3 - t : 7 - t]
            shares = [shares[k] + coef[parity, k][None] * total for k in range(5)]
        for k in range(5):
            gbuf[k] = shares[k]
        result = jnp.zeros((4, 8, 128), F32)
        for k in range(5):
            result = result + gbuf[k, :, 4 - k : 12 - k, :]
        return result

    def split_rows(parity, kind):
        at = pl.ds(4 + parity, 16, stride=2)
        return jnp.stack([wext[2 * b + kind, at, :] for b in range(7)])

    def fine_field(phase):
        def field(parity):
            along = jnp.zeros((10, 16, 128), F32)
            for k in range(5):
                along = along + coef[parity, k][None] * zext[phase, :, 4 + k : 20 + k, :]
            found = []
            for kind, taps in enumerate((ODD_TAPS, EVEN_TAPS)):
                total = taps[0] * along[0:7]
                for t in range(1, 4):
                    total = total + taps[t] * along[t : t + 7]
                found.append(wsplit[parity, kind] * total)
            return found

        return field

    first_lanes = lax.broadcasted_iota(jnp.int32, (4, 8, 128), 2) < LEV

    def split_pair(j, y):
        at = j * 256 if isinstance(j, int) else pl.multiple_of(j * 256, 256)
        e0 = ens[:, :, pl.ds(at, 128)].astype(F32)
        e1 = ens[:, :, pl.ds(at + 128, 128)].astype(F32)
        p0, p1 = e0 * y, e1 * y
        kept = jnp.where(first_lanes, p0, p1)
        moved = jnp.where(first_lanes, p1, p0)
        total = (kept + pltpu.roll(moved, LEV, 2)).reshape(32, 128)
        high = total.astype(BF16)
        low = (total - high.astype(F32)).astype(BF16)
        return e0, e1, high, low

    def combine_spread(y):
        acc = jnp.zeros((4, 8, 128), F32)
        for j in range(PAIRS):
            e0, e1, high, low = split_pair(j, y)
            both = jnp.concatenate([high, low], axis=0)
            main = jnp.dot(both, sq_hi[j], preferred_element_type=F32)
            rest = jnp.dot(high, sq_lo[j], preferred_element_type=F32)
            out = (main[:32] + (main[32:] + rest)).reshape(4, 8, 128)
            turned = pltpu.roll(out, LEV, 2)
            acc = acc + e0 * jnp.where(first_lanes, out, turned)
            acc = acc + e1 * jnp.where(first_lanes, turned, out)
        return acc

    def spread(which):
        y = yv[which]

        def body(step, carry):
            for extra in range(UNROLL):
                j = step * UNROLL + extra
                _, _, high, low = split_pair(j, y)
                both = jnp.concatenate([high, low], axis=0)
                main = jnp.dot(both, tents[j], preferred_element_type=F32)
                out = (main[:32] + main[32:]).reshape(4, 8, 128) * inv2[j][None]
                uvec[which, :, :, pl.ds(pl.multiple_of(j * 128, 128), 128)] = out
            return carry

        lax.fori_loop(0, PAIRS // UNROLL, body, 0)

    own_e.wait()
    for dlat, dlon in DIRECTIONS:
        inside(-dlat, lambda dlat=dlat, dlon=dlon: share_copy(dlat, dlon).wait_recv())
    start = ybuf[2:6, 8:16, :]
    for number in range(8):
        start = start + yin[number]
    yv[0] = start

    for phase in range(2):
        z = combine_spread(yv[phase])
        zext[phase, 3:7, 8:16, :] = z
        for dlat, dlon in DIRECTIONS:

            def send(dlat=dlat, dlon=dlon, phase=phase):
                z_copy(phase, dlat, dlon).start()

            inside(dlat, send)
        spread(phase)
        if phase == 0:
            for dlat in (-1, 1):
                inside(-dlat, lambda dlat=dlat: param_copy(dlat).wait_recv())
            find_coef((0, 1, 2))
            for dlat, dlon in DIRECTIONS:
                inside(-dlat, lambda dlat=dlat, dlon=dlon: weight_copy(dlat, dlon).wait_recv())
            for parity in range(2):
                for kind in range(2):
                    wsplit[parity, kind] = split_rows(parity, kind)
        for dlat, dlon in DIRECTIONS:

            def receive(dlat=dlat, dlon=dlon, phase=phase):
                z_copy(phase, dlat, dlon).wait_recv()

            inside(-dlat, receive)
        yv[phase + 1] = restrict(fine_field(phase))

    lane1 = lax.broadcasted_iota(jnp.int32, (1, 128), 1)
    local = jnp.zeros((1, 128), F32)
    for number, (left, right) in enumerate(((0, 0), (0, 1), (1, 1), (0, 2), (1, 2))):
        plane = jnp.sum(zext[left, 3:7, 8:16, :] * yv[right], axis=0)
        value = jnp.sum(jnp.sum(plane, axis=0, keepdims=True), axis=1, keepdims=True)
        local = local + jnp.where(lane1 == number, jnp.broadcast_to(value, (1, 128)), 0.0)

    for number, (me, count, device, slots, send_sems, recv_sems) in enumerate(stages):

        def stage_copy(target, slot):
            return pltpu.make_async_remote_copy(
                src_ref=slots.at[me],
                dst_ref=slots.at[slot],
                send_sem=send_sems.at[target],
                recv_sem=recv_sems.at[slot],
                device_id=device(target),
                device_id_type=MESH,
            )

        slots[me] = local
        for step in range(1, count):
            stage_copy(lax.rem(me + step, count), me).start()
        if number == 0:
            spread(2)
        for step in range(1, count):
            other = lax.rem(me + step, count)
            stage_copy(other, other).wait_recv()
        local = slots[0]
        for slot in range(1, count):
            local = local + slots[slot]

    def picked(number):
        one = jnp.sum(jnp.where(lane1 == number, local, 0.0), axis=1, keepdims=True)
        return jnp.broadcast_to(one, (8, 128))

    a, b, d, e, f = (picked(number) for number in range(5))
    beta0 = jnp.sqrt(a / entries + EPSILON)
    alpha0 = (a + b) / (entries * beta0 * beta0)
    rest = 1.0 - alpha0
    square = (rest * rest * a + 2.0 * rest * b + d) / (beta0 * beta0)
    beta1 = jnp.sqrt(square / entries + EPSILON)
    mixed = (rest * rest * b + rest * (d + e) + f) / (beta0 * beta0)
    alpha1 = (square + mixed) / (entries * beta1 * beta1)
    back = ((rest * a + b) + (rest * b + e)) / (entries * beta0 * beta0 * beta1)
    scale = 1.0 / (beta0 * beta1)
    q2 = scale
    q1 = (1.0 + rest - alpha1) * scale
    q0 = (rest - alpha1 * rest) * scale - back / beta0
    row8 = lax.broadcasted_iota(jnp.int32, (8, 128), 0)
    left = lax.broadcasted_iota(jnp.int32, (8, 128), 1) == 0
    table = jnp.where(row8 == 0, jnp.where(left, alpha0, alpha1), jnp.where(left, beta0, beta1))
    for number, q in enumerate((q0, q1, q2)):
        table = jnp.where(row8 == 2 + number, q, table)
    table_out[...] = table

    for dlat in (-1, 1):
        inside(dlat, lambda dlat=dlat: param_copy(dlat).wait_send())
    for dlat, dlon in DIRECTIONS:

        def drain(dlat=dlat, dlon=dlon):
            share_copy(dlat, dlon).wait_send()
            weight_copy(dlat, dlon).wait_send()
            z_copy(0, dlat, dlon).wait_send()
            z_copy(1, dlat, dlon).wait_send()

        inside(dlat, drain)
    for me, count, device, slots, send_sems, recv_sems in stages:
        for step in range(1, count):
            target = lax.rem(me + step, count)
            pltpu.make_async_remote_copy(
                src_ref=slots.at[me],
                dst_ref=slots.at[me],
                send_sem=send_sems.at[target],
                recv_sem=recv_sems.at[me],
                device_id=device(target),
                device_id_type=MESH,
            ).wait_send()


def finish(table, u, coef_hbm, vec_hbm, corner, vec, sems):
    corner[...] = table[0:2, 0:2]
    tail = pltpu.make_async_copy(corner, coef_hbm, sems.at[4])
    tail.start()
    stores = [pltpu.make_async_copy(vec.at[c], vec_hbm.at[c], sems.at[c]) for c in range(4)]
    q = [jnp.broadcast_to(table[2 + k : 3 + k, :], (8, 128)) for k in range(3)]
    wide = [jnp.concatenate([part] * 8, axis=1) for part in q]
    for c in range(4):
        for step in range(M * LEV // 1024):
            at = slice(step * 1024, (step + 1) * 1024)
            vec[c, :, at] = (
                wide[0] * u[0, c, :, at] + wide[1] * u[1, c, :, at] + wide[2] * u[2, c, :, at]
            ).astype(BF16)
        stores[c].start()
    for store in stores:
        store.wait()
    tail.wait()


def per_device(topo, ensemble, innovation, obs_weight, lat_offset, lat_weight, band_widths):
    zh_n, x_n, zl_n, y_n, core_n = topo
    entries = float(4 * 8 * M * LEV * zh_n * x_n * zl_n * y_n * core_n)
    vmem = pltpu.VMEM
    dma = pltpu.SemaphoreType.DMA
    group_a, group_b, group_c = x_n * core_n, y_n, zh_n * zl_n
    anywhere = pl.BlockSpec(memory_space=pl.ANY)
    in_vmem = pl.BlockSpec(memory_space=pltpu.VMEM)
    table, u = pl.pallas_call(
        functools.partial(kernel, topo, entries),
        out_shape=(
            jax.ShapeDtypeStruct((8, 128), F32),
            jax.ShapeDtypeStruct((3, 4, 8, M * LEV), F32),
        ),
        in_specs=[
            anywhere,
            anywhere,
            anywhere,
            anywhere,
            anywhere,
            anywhere,
        ],
        out_specs=(in_vmem, in_vmem),
        scratch_shapes=[
            vmem((1, 16), jnp.int32),
            vmem((1, 16), F32),
            pltpu.SMEM((1, M), jnp.int32),
            vmem((4, 8, 2 * M * LEV), BF16),
            vmem((8, 16, 128), F32),
            vmem((8, 40, 128), F32),
            vmem((5, 8, 32, 128), F32),
            vmem((8, 24, 128), F32),
            vmem((8, 4, 8, 128), F32),
            vmem((14, 40, 128), F32),
            vmem((2, 2, 7, 16, 128), F32),
            vmem((2, 10, 24, 128), F32),
            vmem((3, 4, 8, 128), F32),
            vmem((3, 8, 128), F32),
            vmem((2, 5, 16, 128), F32),
            vmem((5, 4, 16, 128), F32),
            vmem((PAIRS, 128, 128), BF16),
            vmem((PAIRS, 128, 128), BF16),
            vmem((PAIRS, 128, 128), BF16),
            vmem((PAIRS, 8, 128), F32),
            vmem((group_a, 1, 128), F32),
            vmem((group_b, 1, 128), F32),
            vmem((group_c, 1, 128), F32),
            dma((6,)),
            dma((2, 8)),
            dma((2, 8)),
            dma((2,)),
            dma((2,)),
            dma((2, 8)),
            dma((2, 8)),
            dma((group_a,)),
            dma((group_a,)),
            dma((group_b,)),
            dma((group_b,)),
            dma((group_c,)),
            dma((group_c,)),
        ],
        compiler_params=pltpu.CompilerParams(
            collective_id=0, has_side_effects=True, vmem_limit_bytes=24 * 1024 * 1024
        ),
        name="lanczos",
    )(
        *(
            pltpu.with_memory_space_constraint(value, pltpu.HBM)
            for value in (
                ensemble,
                innovation,
                obs_weight,
                lat_offset.reshape(1, 16),
                lat_weight.reshape(1, 16),
                band_widths.reshape(1, M),
            )
        )
    )
    return pl.pallas_call(
        finish,
        out_shape=(
            jax.ShapeDtypeStruct((2, 2), F32),
            jax.ShapeDtypeStruct((4, 8, M * LEV), BF16),
        ),
        in_specs=[in_vmem, in_vmem],
        out_specs=(anywhere, anywhere),
        scratch_shapes=[
            vmem((2, 2), F32),
            vmem((4, 8, M * LEV), BF16),
            dma((5,)),
        ],
        compiler_params=pltpu.CompilerParams(vmem_limit_bytes=16 * 1024 * 1024),
        name="finish",
    )(table, u)


def solution(mesh):
    return jax.shard_map(
        functools.partial(per_device, TOPO),
        mesh=mesh,
        in_specs=(
            P("lon", "lat", None),
            P("lon", "lat", None),
            P("lon", "lat", None),
            P("lat"),
            P("lat"),
            P(),
        ),
        out_specs=(P(), P("lon", "lat", None)),
        check_vma=False,
    )
```

```python
import functools

import jax
import jax.numpy as jnp
from jax import lax
from jax.experimental import pallas as pl
from jax.experimental.pallas import tpu as pltpu
from jax.sharding import PartitionSpec as P

M = 80
LEV = 64
PAIRS = M // 2
EVEN_TAPS = (-0.0234375, 0.2265625, 0.8671875, -0.0703125)
ODD_TAPS = (-0.0703125, 0.8671875, 0.2265625, -0.0234375)
EPSILON = 1e-06
F32 = jnp.float32
BF16 = jnp.bfloat16
MESH = pl.DeviceIdType.MESH
TOPO = (4, 4, 3, 8, 2)
DIRECTIONS = ((1, 1), (1, -1), (-1, 1), (-1, -1), (1, 0), (-1, 0), (0, 1), (0, -1))
UNROLL = 8


def kernel(
    topo,
    entries,
    ens_hbm,
    innov_hbm,
    wobs_hbm,
    offset_hbm,
    weight_hbm,
    bands_hbm,
    table_out,
    uvec,
    offset_ref,
    weight_ref,
    bands_ref,
    ens,
    down,
    fown,
    hbuf,
    ybuf,
    yin,
    wown,
    wext,
    wsplit,
    zext,
    yv,
    params,
    coef,
    gbuf,
    tents,
    sq_hi,
    sq_lo,
    inv2,
    red_a,
    red_b,
    red_c,
    local_sem,
    in_send,
    in_recv,
    par_send,
    par_recv,
    z_send,
    z_recv,
    a_send,
    a_recv,
    b_send,
    b_recv,
    c_send,
    c_recv,
):
    zh_n, x_n, zl_n, y_n, core_n = topo
    lat_n, lon_n = zh_n * x_n, zl_n * y_n * core_n
    lat, lon = lax.axis_index("lat"), lax.axis_index("lon")
    z_hi, x = lat // x_n, lat % x_n
    z_lo, y_core = lon // (y_n * core_n), lon % (y_n * core_n)
    y_pos, core = y_core // core_n, y_core % core_n

    def neighbour(dlat, dlon):
        return (lat + dlat, lax.rem(lon + dlon + lon_n, lon_n))

    def inside(dlat, body):
        if dlat == 0:
            body()
        else:
            pl.when((lat + dlat >= 0) & (lat + dlat < lat_n))(body)

    def steps(count):
        return sorted(range(1, count), key=lambda step: -min(step, count - step))

    def dev_a(i):
        return (z_hi * x_n + i // core_n, lon - core + i % core_n)

    def dev_b(i):
        return (lat, z_lo * (y_n * core_n) + i * core_n + core)

    def dev_c(i):
        return ((i // zl_n) * x_n + x, (i % zl_n) * (y_n * core_n) + y_core)

    stages = (
        (x * core_n + core, x_n * core_n, dev_a, red_a, a_send, a_recv),
        (y_pos, y_n, dev_b, red_b, b_send, b_recv),
        (z_hi * zl_n + z_lo, zh_n * zl_n, dev_c, red_c, c_send, c_recv),
    )

    small = [
        pltpu.make_async_copy(src, dst, local_sem.at[3 + number])
        for number, (src, dst) in enumerate(
            ((bands_hbm, bands_ref), (weight_hbm, weight_ref), (offset_hbm, offset_ref))
        )
    ]
    own_d = pltpu.make_async_copy(innov_hbm, down, local_sem.at[0])
    own_w = pltpu.make_async_copy(wobs_hbm, wown, local_sem.at[1])
    own_e = pltpu.make_async_copy(ens_hbm, ens, local_sem.at[2])
    own_d.start()
    own_w.start()
    for copy in small:
        copy.start()

    yin[...] = jnp.zeros(yin.shape, F32)
    wext[...] = jnp.zeros(wext.shape, F32)
    zext[...] = jnp.zeros(zext.shape, F32)
    params[...] = jnp.zeros(params.shape, F32)

    barrier = pltpu.get_barrier_semaphore()
    for dlat, dlon in DIRECTIONS:

        def greet(dlat=dlat, dlon=dlon):
            pl.semaphore_signal(
                barrier, inc=1, device_id=neighbour(dlat, dlon), device_id_type=MESH
            )

        inside(dlat, greet)
    for me, count, device, _, _, _ in reversed(stages):
        for step in steps(count):
            pl.semaphore_signal(
                barrier,
                inc=1,
                device_id=device(lax.rem(me + step, count)),
                device_id_type=MESH,
            )

    own_e.start()
    fown[...] = jnp.zeros(fown.shape, F32)
    hbuf[...] = jnp.zeros(hbuf.shape, F32)
    for copy in small:
        copy.wait()
    params[1, 0:1, 0:16] = weight_ref[...]
    params[1, 1:2, 0:16] = offset_ref[...].astype(F32)

    own_d.wait()
    own_w.wait()
    fown[:, 8:24, :] = down[...] * wown[...]
    wext[3:11, 8:24, :] = wown[...]

    row = lax.broadcasted_iota(jnp.int32, (16, 128), 0)
    lane = lax.broadcasted_iota(jnp.int32, (16, 128), 1)

    def find_coef(sources):
        for parity in range(2):
            fine = 2 * row - 4 + parity
            picked = []
            for kind in range(2):
                total = jnp.zeros((16, 128), F32)
                for source in sources:
                    line = jnp.broadcast_to(params[source, kind : kind + 1, :], (16, 128))
                    total = total + jnp.where(lane == fine + 16 - 16 * source, line, 0.0)
                picked.append(
                    jnp.broadcast_to(jnp.sum(total, axis=1, keepdims=True), (16, 128))
                )
            upper, offset = picked
            for k in range(5):
                coef[parity, k] = jnp.where(offset == float(k), 1.0 - upper, 0.0) + jnp.where(
                    offset == float(k - 1), upper, 0.0
                )

    find_coef((1,))
    shares = [jnp.zeros((8, 16, 128), F32) for _ in range(5)]
    for parity in range(2):
        at = pl.ds(4 + parity, 16, stride=2)
        columns = [jnp.zeros((16, 128), F32) for _ in range(8)]
        for c in range(4):
            even, odd = fown[2 * c, at, :], fown[2 * c + 1, at, :]
            for t in range(4):
                columns[c + t] = columns[c + t] + EVEN_TAPS[t] * even
                columns[c + 1 + t] = columns[c + 1 + t] + ODD_TAPS[t] * odd
        along = jnp.stack(columns)
        shares = [shares[k] + coef[parity, k][None] * along for k in range(5)]
    for k in range(5):
        hbuf[k, :, 8:24, :] = shares[k]
    total = jnp.zeros((8, 24, 128), F32)
    for k in range(5):
        total = total + hbuf[k, :, 4 - k : 28 - k, :]
    ybuf[...] = total

    edges = (lat == 0).astype(jnp.int32) + (lat == lat_n - 1).astype(jnp.int32)
    others = sum(count - 1 for _, count, _, _, _, _ in stages)
    pl.semaphore_wait(barrier, others + 8 - 3 * edges)

    def cut(delta, size, width, before):
        if delta == 0:
            return slice(0, size), slice(before, before + size)
        if delta == 1:
            return slice(size - width, size), slice(before - width, before)
        return slice(0, width), slice(before + size, before + size + width)

    def shifted(part, by):
        return slice(part.start + by, part.stop + by)

    def weight_copy(dlat, dlon):
        src_cols, dst_cols = cut(dlon, 8, 3, 3)
        src_rows, dst_rows = cut(dlat, 16, 4, 8)
        number = DIRECTIONS.index((dlat, dlon))
        return pltpu.make_async_remote_copy(
            src_ref=wobs_hbm.at[src_cols, src_rows],
            dst_ref=wext.at[dst_cols, dst_rows],
            send_sem=in_send.at[1, number],
            recv_sem=in_recv.at[1, number],
            device_id=neighbour(dlat, dlon),
            device_id_type=MESH,
        )

    def share_copy(dlat, dlon):
        number = DIRECTIONS.index((dlat, dlon))
        src_cols, dst_cols = (
            (slice(2, 6), slice(0, 4)),
            (slice(6, 8), slice(0, 2)),
            (slice(0, 2), slice(2, 4)),
        )[dlon]
        src_rows, dst_rows = (
            (slice(8, 16), slice(0, 8)),
            (slice(16, 18), slice(0, 2)),
            (slice(6, 8), slice(6, 8)),
        )[dlat]
        return pltpu.make_async_remote_copy(
            src_ref=ybuf.at[src_cols, src_rows],
            dst_ref=yin.at[number, dst_cols, dst_rows],
            send_sem=in_send.at[0, number],
            recv_sem=in_recv.at[0, number],
            device_id=neighbour(dlat, dlon),
            device_id_type=MESH,
        )

    def param_copy(dlat):
        return pltpu.make_async_remote_copy(
            src_ref=params.at[1],
            dst_ref=params.at[1 - dlat],
            send_sem=par_send.at[(dlat + 1) // 2],
            recv_sem=par_recv.at[(dlat + 1) // 2],
            device_id=neighbour(dlat, 0),
            device_id_type=MESH,
        )

    def z_copy(phase, dlat, dlon):
        src_cols, dst_cols = cut(dlon, 4, 3, 3)
        src_rows, dst_rows = cut(dlat, 8, 4, 8)
        number = DIRECTIONS.index((dlat, dlon))
        return pltpu.make_async_remote_copy(
            src_ref=zext.at[phase, shifted(src_cols, 3), shifted(src_rows, 8)],
            dst_ref=zext.at[phase, dst_cols, dst_rows],
            send_sem=z_send.at[phase, number],
            recv_sem=z_recv.at[phase, number],
            device_id=neighbour(dlat, dlon),
            device_id_type=MESH,
        )

    for dlat, dlon in DIRECTIONS:
        inside(dlat, lambda dlat=dlat, dlon=dlon: share_copy(dlat, dlon).start())
    for dlat in (-1, 1):
        inside(dlat, lambda dlat=dlat: param_copy(dlat).start())
    for dlat, dlon in DIRECTIONS:
        inside(dlat, lambda dlat=dlat, dlon=dlon: weight_copy(dlat, dlon).start())

    rows = lax.broadcasted_iota(jnp.int32, (128, 128), 0)
    cols = lax.broadcasted_iota(jnp.int32, (128, 128), 1)
    same = (rows < LEV) == (cols < LEV)
    distance = jnp.where(same, jnp.abs(rows - cols), 1000)
    first_half = lax.broadcasted_iota(jnp.int32, (1, 128), 1) < LEV

    def build(j):
        width = jnp.where(first_half, bands_ref[0, 2 * j] + 1, bands_ref[0, 2 * j + 1] + 1)
        tent = jnp.maximum(width - distance, 0).astype(F32).astype(BF16)
        wide = width.astype(F32)
        scale = 1.0 / (wide * wide)
        square = jnp.dot(tent, tent, preferred_element_type=F32) * (scale * scale)
        high = square.astype(BF16)
        tents[j] = tent
        sq_hi[j] = high
        sq_lo[j] = (square - high.astype(F32)).astype(BF16)
        inv2[j] = jnp.broadcast_to(scale, (8, 128))

    def build_some(step, carry):
        for extra in range(UNROLL):
            build(step * UNROLL + extra)
        return carry

    lax.fori_loop(0, PAIRS // UNROLL, build_some, 0)

    def restrict(fields):
        shares = [jnp.zeros((4, 16, 128), F32) for _ in range(5)]
        for parity in range(2):
            odd, even = fields(parity)
            total = jnp.zeros((4, 16, 128), F32)
            for t in range(4):
                total = total + ODD_TAPS[t] * odd[3 - t : 7 - t] + EVEN_TAPS[t] * even[3 - t : 7 - t]
            shares = [shares[k] + coef[parity, k][None] * total for k in range(5)]
        for k in range(5):
            gbuf[k] = shares[k]
        result = jnp.zeros((4, 8, 128), F32)
        for k in range(5):
            result = result + gbuf[k, :, 4 - k : 12 - k, :]
        return result

    def split_rows(parity, kind):
        at = pl.ds(4 + parity, 16, stride=2)
        return jnp.stack([wext[2 * b + kind, at, :] for b in range(7)])

    def fine_field(phase):
        def field(parity):
            along = jnp.zeros((10, 16, 128), F32)
            for k in range(5):
                along = along + coef[parity, k][None] * zext[phase, :, 4 + k : 20 + k, :]
            found = []
            for kind, taps in enumerate((ODD_TAPS, EVEN_TAPS)):
                total = taps[0] * along[0:7]
                for t in range(1, 4):
                    total = total + taps[t] * along[t : t + 7]
                found.append(wsplit[parity, kind] * total)
            return found

        return field

    first_lanes = lax.broadcasted_iota(jnp.int32, (4, 8, 128), 2) < LEV

    def split_pair(j, y):
        at = j * 256 if isinstance(j, int) else pl.multiple_of(j * 256, 256)
        e0 = ens[:, :, pl.ds(at, 128)].astype(F32)
        e1 = ens[:, :, pl.ds(at + 128, 128)].astype(F32)
        p0, p1 = e0 * y, e1 * y
        kept = jnp.where(first_lanes, p0, p1)
        moved = jnp.where(first_lanes, p1, p0)
        total = (kept + pltpu.roll(moved, LEV, 2)).reshape(32, 128)
        high = total.astype(BF16)
        low = (total - high.astype(F32)).astype(BF16)
        return e0, e1, high, low

    def combine_spread(y):
        acc = jnp.zeros((4, 8, 128), F32)
        for j in range(PAIRS):
            e0, e1, high, low = split_pair(j, y)
            both = jnp.concatenate([high, low], axis=0)
            main = jnp.dot(both, sq_hi[j], preferred_element_type=F32)
            rest = jnp.dot(high, sq_lo[j], preferred_element_type=F32)
            out = (main[:32] + (main[32:] + rest)).reshape(4, 8, 128)
            turned = pltpu.roll(out, LEV, 2)
            acc = acc + e0 * jnp.where(first_lanes, out, turned)
            acc = acc + e1 * jnp.where(first_lanes, turned, out)
        return acc

    def spread(which):
        y = yv[which]

        def body(step, carry):
            for extra in range(UNROLL):
                j = step * UNROLL + extra
                _, _, high, low = split_pair(j, y)
                both = jnp.concatenate([high, low], axis=0)
                main = jnp.dot(both, tents[j], preferred_element_type=F32)
                out = (main[:32] + main[32:]).reshape(4, 8, 128) * inv2[j][None]
                uvec[which, :, :, pl.ds(pl.multiple_of(j * 128, 128), 128)] = out
            return carry

        lax.fori_loop(0, PAIRS // UNROLL, body, 0)

    own_e.wait()
    for dlat, dlon in DIRECTIONS:
        inside(-dlat, lambda dlat=dlat, dlon=dlon: share_copy(dlat, dlon).wait_recv())
    start = ybuf[2:6, 8:16, :]
    for number in range(8):
        start = start + yin[number]
    yv[0] = start

    for phase in range(2):
        z = combine_spread(yv[phase])
        zext[phase, 3:7, 8:16, :] = z
        for dlat, dlon in DIRECTIONS:

            def send(dlat=dlat, dlon=dlon, phase=phase):
                z_copy(phase, dlat, dlon).start()

            inside(dlat, send)
        spread(phase)
        if phase == 0:
            for dlat in (-1, 1):
                inside(-dlat, lambda dlat=dlat: param_copy(dlat).wait_recv())
            find_coef((0, 1, 2))
            for dlat, dlon in DIRECTIONS:
                inside(-dlat, lambda dlat=dlat, dlon=dlon: weight_copy(dlat, dlon).wait_recv())
            for parity in range(2):
                for kind in range(2):
                    wsplit[parity, kind] = split_rows(parity, kind)
        for dlat, dlon in DIRECTIONS:

            def receive(dlat=dlat, dlon=dlon, phase=phase):
                z_copy(phase, dlat, dlon).wait_recv()

            inside(-dlat, receive)
        yv[phase + 1] = restrict(fine_field(phase))

    lane1 = lax.broadcasted_iota(jnp.int32, (1, 128), 1)
    local = jnp.zeros((1, 128), F32)
    for number, (left, right) in enumerate(((0, 0), (0, 1), (1, 1), (0, 2), (1, 2))):
        plane = jnp.sum(zext[left, 3:7, 8:16, :] * yv[right], axis=0)
        value = jnp.sum(jnp.sum(plane, axis=0, keepdims=True), axis=1, keepdims=True)
        local = local + jnp.where(lane1 == number, jnp.broadcast_to(value, (1, 128)), 0.0)

    for number, (me, count, device, slots, send_sems, recv_sems) in enumerate(stages):

        def stage_copy(target, slot):
            return pltpu.make_async_remote_copy(
                src_ref=slots.at[me],
                dst_ref=slots.at[slot],
                send_sem=send_sems.at[target],
                recv_sem=recv_sems.at[slot],
                device_id=device(target),
                device_id_type=MESH,
            )

        slots[me] = local
        for step in steps(count):
            stage_copy(lax.rem(me + step, count), me).start()
        if number == 0:
            spread(2)
        for step in steps(count):
            other = lax.rem(me + step, count)
            stage_copy(other, other).wait_recv()
        local = slots[0]
        for slot in range(1, count):
            local = local + slots[slot]

    def picked(number):
        one = jnp.sum(jnp.where(lane1 == number, local, 0.0), axis=1, keepdims=True)
        return jnp.broadcast_to(one, (8, 128))

    a, b, d, e, f = (picked(number) for number in range(5))
    square0 = a * (1.0 / entries) + EPSILON
    inverse0 = 1.0 / square0
    alpha0 = (a + b) * (inverse0 * (1.0 / entries))
    rest = 1.0 - alpha0
    own1 = (rest * (rest * a) + 2.0 * (rest * b) + d) * inverse0
    square1 = own1 * (1.0 / entries) + EPSILON
    inverse1 = 1.0 / square1
    mixed = (rest * (rest * b) + rest * (d + e) + f) * inverse0
    alpha1 = (own1 + mixed) * (inverse1 * (1.0 / entries))
    back = ((rest * a + b) + (rest * b + e)) * (inverse0 * (1.0 / entries))
    beta0, beta1 = jnp.sqrt(square0), jnp.sqrt(square1)
    q2 = jnp.sqrt(inverse0 * inverse1)
    q1 = (1.0 + rest - alpha1) * q2
    q0 = (rest - alpha1 * rest - back) * q2
    row8 = lax.broadcasted_iota(jnp.int32, (8, 128), 0)
    left = lax.broadcasted_iota(jnp.int32, (8, 128), 1) == 0
    table = jnp.where(row8 == 0, jnp.where(left, alpha0, alpha1), jnp.where(left, beta0, beta1))
    for number, q in enumerate((q0, q1, q2)):
        table = jnp.where(row8 == 2 + number, q, table)
    table_out[...] = table

    for dlat in (-1, 1):
        inside(dlat, lambda dlat=dlat: param_copy(dlat).wait_send())
    for dlat, dlon in DIRECTIONS:

        def drain(dlat=dlat, dlon=dlon):
            share_copy(dlat, dlon).wait_send()
            weight_copy(dlat, dlon).wait_send()
            z_copy(0, dlat, dlon).wait_send()
            z_copy(1, dlat, dlon).wait_send()

        inside(dlat, drain)
    for me, count, device, slots, send_sems, recv_sems in stages:
        for step in steps(count):
            target = lax.rem(me + step, count)
            pltpu.make_async_remote_copy(
                src_ref=slots.at[me],
                dst_ref=slots.at[me],
                send_sem=send_sems.at[target],
                recv_sem=recv_sems.at[me],
                device_id=device(target),
                device_id_type=MESH,
            ).wait_send()


def finish(table, u, coef_hbm, vec_hbm, corner, vec, sems):
    corner[...] = table[0:2, 0:2]
    tail = pltpu.make_async_copy(corner, coef_hbm, sems.at[4])
    tail.start()
    stores = [pltpu.make_async_copy(vec.at[c], vec_hbm.at[c], sems.at[c]) for c in range(4)]
    q = [jnp.broadcast_to(table[2 + k : 3 + k, :], (8, 128)) for k in range(3)]
    wide = [jnp.concatenate([part] * 8, axis=1) for part in q]
    for c in range(4):
        for step in range(M * LEV // 1024):
            at = slice(step * 1024, (step + 1) * 1024)
            vec[c, :, at] = (
                wide[0] * u[0, c, :, at] + wide[1] * u[1, c, :, at] + wide[2] * u[2, c, :, at]
            ).astype(BF16)
        stores[c].start()
    for store in stores:
        store.wait()
    tail.wait()


def per_device(topo, ensemble, innovation, obs_weight, lat_offset, lat_weight, band_widths):
    zh_n, x_n, zl_n, y_n, core_n = topo
    entries = float(4 * 8 * M * LEV * zh_n * x_n * zl_n * y_n * core_n)
    vmem = pltpu.VMEM
    dma = pltpu.SemaphoreType.DMA
    group_a, group_b, group_c = x_n * core_n, y_n, zh_n * zl_n
    anywhere = pl.BlockSpec(memory_space=pl.ANY)
    in_vmem = pl.BlockSpec(memory_space=pltpu.VMEM)
    table, u = pl.pallas_call(
        functools.partial(kernel, topo, entries),
        out_shape=(
            jax.ShapeDtypeStruct((8, 128), F32),
            jax.ShapeDtypeStruct((3, 4, 8, M * LEV), F32),
        ),
        in_specs=[
            anywhere,
            anywhere,
            anywhere,
            anywhere,
            anywhere,
            anywhere,
        ],
        out_specs=(in_vmem, in_vmem),
        scratch_shapes=[
            vmem((1, 16), jnp.int32),
            vmem((1, 16), F32),
            pltpu.SMEM((1, M), jnp.int32),
            vmem((4, 8, 2 * M * LEV), BF16),
            vmem((8, 16, 128), F32),
            vmem((8, 40, 128), F32),
            vmem((5, 8, 32, 128), F32),
            vmem((8, 24, 128), F32),
            vmem((8, 4, 8, 128), F32),
            vmem((8, 16, 128), F32),
            vmem((14, 40, 128), F32),
            vmem((2, 2, 7, 16, 128), F32),
            vmem((2, 10, 24, 128), F32),
            vmem((3, 4, 8, 128), F32),
            vmem((3, 8, 128), F32),
            vmem((2, 5, 16, 128), F32),
            vmem((5, 4, 16, 128), F32),
            vmem((PAIRS, 128, 128), BF16),
            vmem((PAIRS, 128, 128), BF16),
            vmem((PAIRS, 128, 128), BF16),
            vmem((PAIRS, 8, 128), F32),
            vmem((group_a, 1, 128), F32),
            vmem((group_b, 1, 128), F32),
            vmem((group_c, 1, 128), F32),
            dma((6,)),
            dma((2, 8)),
            dma((2, 8)),
            dma((2,)),
            dma((2,)),
            dma((2, 8)),
            dma((2, 8)),
            dma((group_a,)),
            dma((group_a,)),
            dma((group_b,)),
            dma((group_b,)),
            dma((group_c,)),
            dma((group_c,)),
        ],
        compiler_params=pltpu.CompilerParams(
            collective_id=0, has_side_effects=True, vmem_limit_bytes=24 * 1024 * 1024
        ),
        name="lanczos",
    )(
        *(
            pltpu.with_memory_space_constraint(value, pltpu.HBM)
            for value in (
                ensemble,
                innovation,
                obs_weight,
                lat_offset.reshape(1, 16),
                lat_weight.reshape(1, 16),
                band_widths.reshape(1, M),
            )
        )
    )
    return pl.pallas_call(
        finish,
        out_shape=(
            jax.ShapeDtypeStruct((2, 2), F32),
            jax.ShapeDtypeStruct((4, 8, M * LEV), BF16),
        ),
        in_specs=[in_vmem, in_vmem],
        out_specs=(anywhere, anywhere),
        scratch_shapes=[
            vmem((2, 2), F32),
            vmem((4, 8, M * LEV), BF16),
            dma((5,)),
        ],
        compiler_params=pltpu.CompilerParams(vmem_limit_bytes=16 * 1024 * 1024),
        name="finish",
    )(table, u)


def solution(mesh):
    return jax.shard_map(
        functools.partial(per_device, TOPO),
        mesh=mesh,
        in_specs=(
            P("lon", "lat", None),
            P("lon", "lat", None),
            P("lon", "lat", None),
            P("lat"),
            P("lat"),
            P(),
        ),
        out_specs=(P(), P("lon", "lat", None)),
        check_vma=False,
    )
```

```python
import functools

import jax
import jax.numpy as jnp
from jax import lax
from jax.experimental import pallas as pl
from jax.experimental.pallas import tpu as pltpu
from jax.sharding import PartitionSpec as P

M = 80
LEV = 64
PAIRS = M // 2
EVEN_TAPS = (-0.0234375, 0.2265625, 0.8671875, -0.0703125)
ODD_TAPS = (-0.0703125, 0.8671875, 0.2265625, -0.0234375)
EPSILON = 1e-06
F32 = jnp.float32
BF16 = jnp.bfloat16
MESH = pl.DeviceIdType.MESH
TOPO = (4, 4, 3, 8, 2)
DIRECTIONS = ((1, 1), (1, -1), (-1, 1), (-1, -1), (1, 0), (-1, 0), (0, 1), (0, -1))
UNROLL = 8


def kernel(
    topo,
    entries,
    ens_hbm,
    innov_hbm,
    wobs_hbm,
    offset_hbm,
    weight_hbm,
    bands_hbm,
    table_out,
    uvec,
    offset_ref,
    weight_ref,
    bands_ref,
    ens,
    down,
    fown,
    hbuf,
    ybuf,
    yin,
    wown,
    wext,
    wsplit,
    zext,
    yv,
    params,
    coef,
    gbuf,
    tents,
    sq_hi,
    sq_lo,
    inv2,
    red_a,
    red_b,
    red_c,
    local_sem,
    in_send,
    in_recv,
    par_send,
    par_recv,
    z_send,
    z_recv,
    a_send,
    a_recv,
    b_send,
    b_recv,
    c_send,
    c_recv,
):
    zh_n, x_n, zl_n, y_n, core_n = topo
    lat_n, lon_n = zh_n * x_n, zl_n * y_n * core_n
    lat, lon = lax.axis_index("lat"), lax.axis_index("lon")
    z_hi, x = lat // x_n, lat % x_n
    z_lo, y_core = lon // (y_n * core_n), lon % (y_n * core_n)
    y_pos, core = y_core // core_n, y_core % core_n

    def neighbour(dlat, dlon):
        return (lat + dlat, lax.rem(lon + dlon + lon_n, lon_n))

    def inside(dlat, body):
        if dlat == 0:
            body()
        else:
            pl.when((lat + dlat >= 0) & (lat + dlat < lat_n))(body)

    def steps(count):
        return sorted(range(1, count), key=lambda step: -min(step, count - step))

    def dev_a(i):
        return (z_hi * x_n + i // core_n, lon - core + i % core_n)

    def dev_b(i):
        return (lat, z_lo * (y_n * core_n) + i * core_n + core)

    def dev_c(i):
        return ((i // zl_n) * x_n + x, (i % zl_n) * (y_n * core_n) + y_core)

    stages = (
        (x * core_n + core, x_n * core_n, dev_a, red_a, a_send, a_recv),
        (y_pos, y_n, dev_b, red_b, b_send, b_recv),
        (z_hi * zl_n + z_lo, zh_n * zl_n, dev_c, red_c, c_send, c_recv),
    )

    small = [
        pltpu.make_async_copy(src, dst, local_sem.at[3 + number])
        for number, (src, dst) in enumerate(
            ((bands_hbm, bands_ref), (weight_hbm, weight_ref), (offset_hbm, offset_ref))
        )
    ]
    own_d = pltpu.make_async_copy(innov_hbm, down, local_sem.at[0])
    own_w = pltpu.make_async_copy(wobs_hbm, wown, local_sem.at[1])
    own_e = pltpu.make_async_copy(ens_hbm, ens, local_sem.at[2])
    own_d.start()
    own_w.start()
    for copy in small:
        copy.start()

    yin[...] = jnp.zeros(yin.shape, F32)
    wext[...] = jnp.zeros(wext.shape, F32)
    zext[...] = jnp.zeros(zext.shape, F32)
    params[...] = jnp.zeros(params.shape, F32)

    barrier = pltpu.get_barrier_semaphore()
    for dlat, dlon in DIRECTIONS:

        def greet(dlat=dlat, dlon=dlon):
            pl.semaphore_signal(
                barrier, inc=1, device_id=neighbour(dlat, dlon), device_id_type=MESH
            )

        inside(dlat, greet)
    for me, count, device, _, _, _ in reversed(stages):
        for step in steps(count):
            pl.semaphore_signal(
                barrier,
                inc=1,
                device_id=device(lax.rem(me + step, count)),
                device_id_type=MESH,
            )

    own_e.start()
    fown[...] = jnp.zeros(fown.shape, F32)
    hbuf[...] = jnp.zeros(hbuf.shape, F32)
    for copy in small:
        copy.wait()
    params[1, 0:1, 0:16] = weight_ref[...]
    params[1, 1:2, 0:16] = offset_ref[...].astype(F32)

    own_d.wait()
    own_w.wait()
    fown[:, 8:24, :] = down[...] * wown[...]
    wext[3:11, 8:24, :] = wown[...]

    row = lax.broadcasted_iota(jnp.int32, (16, 128), 0)
    lane = lax.broadcasted_iota(jnp.int32, (16, 128), 1)

    def find_coef(sources):
        for parity in range(2):
            fine = 2 * row - 4 + parity
            picked = []
            for kind in range(2):
                total = jnp.zeros((16, 128), F32)
                for source in sources:
                    line = jnp.broadcast_to(params[source, kind : kind + 1, :], (16, 128))
                    total = total + jnp.where(lane == fine + 16 - 16 * source, line, 0.0)
                picked.append(
                    jnp.broadcast_to(jnp.sum(total, axis=1, keepdims=True), (16, 128))
                )
            upper, offset = picked
            for k in range(5):
                coef[parity, k] = jnp.where(offset == float(k), 1.0 - upper, 0.0) + jnp.where(
                    offset == float(k - 1), upper, 0.0
                )

    find_coef((1,))
    shares = [jnp.zeros((8, 16, 128), F32) for _ in range(5)]
    for parity in range(2):
        at = pl.ds(4 + parity, 16, stride=2)
        columns = [jnp.zeros((16, 128), F32) for _ in range(8)]
        for c in range(4):
            even, odd = fown[2 * c, at, :], fown[2 * c + 1, at, :]
            for t in range(4):
                columns[c + t] = columns[c + t] + EVEN_TAPS[t] * even
                columns[c + 1 + t] = columns[c + 1 + t] + ODD_TAPS[t] * odd
        along = jnp.stack(columns)
        shares = [shares[k] + coef[parity, k][None] * along for k in range(5)]
    for k in range(5):
        hbuf[k, :, 8:24, :] = shares[k]
    total = jnp.zeros((8, 24, 128), F32)
    for k in range(5):
        total = total + hbuf[k, :, 4 - k : 28 - k, :]
    ybuf[...] = total

    edges = (lat == 0).astype(jnp.int32) + (lat == lat_n - 1).astype(jnp.int32)
    others = sum(count - 1 for _, count, _, _, _, _ in stages)
    pl.semaphore_wait(barrier, others + 8 - 3 * edges)

    def cut(delta, size, width, before):
        if delta == 0:
            return slice(0, size), slice(before, before + size)
        if delta == 1:
            return slice(size - width, size), slice(before - width, before)
        return slice(0, width), slice(before + size, before + size + width)

    def shifted(part, by):
        return slice(part.start + by, part.stop + by)

    def weight_copy(dlat, dlon):
        src_cols, dst_cols = cut(dlon, 8, 3, 3)
        src_rows, dst_rows = cut(dlat, 16, 4, 8)
        number = DIRECTIONS.index((dlat, dlon))
        return pltpu.make_async_remote_copy(
            src_ref=wobs_hbm.at[src_cols, src_rows],
            dst_ref=wext.at[dst_cols, dst_rows],
            send_sem=in_send.at[1, number],
            recv_sem=in_recv.at[1, number],
            device_id=neighbour(dlat, dlon),
            device_id_type=MESH,
        )

    def share_copy(dlat, dlon):
        number = DIRECTIONS.index((dlat, dlon))
        src_cols, dst_cols = (
            (slice(2, 6), slice(0, 4)),
            (slice(6, 8), slice(0, 2)),
            (slice(0, 2), slice(2, 4)),
        )[dlon]
        src_rows, dst_rows = (
            (slice(8, 16), slice(0, 8)),
            (slice(16, 18), slice(0, 2)),
            (slice(6, 8), slice(6, 8)),
        )[dlat]
        return pltpu.make_async_remote_copy(
            src_ref=ybuf.at[src_cols, src_rows],
            dst_ref=yin.at[number, dst_cols, dst_rows],
            send_sem=in_send.at[0, number],
            recv_sem=in_recv.at[0, number],
            device_id=neighbour(dlat, dlon),
            device_id_type=MESH,
        )

    def param_copy(dlat):
        return pltpu.make_async_remote_copy(
            src_ref=params.at[1],
            dst_ref=params.at[1 - dlat],
            send_sem=par_send.at[(dlat + 1) // 2],
            recv_sem=par_recv.at[(dlat + 1) // 2],
            device_id=neighbour(dlat, 0),
            device_id_type=MESH,
        )

    def z_copy(phase, dlat, dlon):
        src_cols, dst_cols = cut(dlon, 4, 3, 3)
        src_rows, dst_rows = cut(dlat, 8, 4, 8)
        number = DIRECTIONS.index((dlat, dlon))
        return pltpu.make_async_remote_copy(
            src_ref=zext.at[phase, shifted(src_cols, 3), shifted(src_rows, 8)],
            dst_ref=zext.at[phase, dst_cols, dst_rows],
            send_sem=z_send.at[phase, number],
            recv_sem=z_recv.at[phase, number],
            device_id=neighbour(dlat, dlon),
            device_id_type=MESH,
        )

    for dlat, dlon in DIRECTIONS:
        inside(dlat, lambda dlat=dlat, dlon=dlon: share_copy(dlat, dlon).start())
    for dlat in (-1, 1):
        inside(dlat, lambda dlat=dlat: param_copy(dlat).start())
    for dlat, dlon in DIRECTIONS:
        inside(dlat, lambda dlat=dlat, dlon=dlon: weight_copy(dlat, dlon).start())

    rows = lax.broadcasted_iota(jnp.int32, (128, 128), 0)
    cols = lax.broadcasted_iota(jnp.int32, (128, 128), 1)
    same = (rows < LEV) == (cols < LEV)
    distance = jnp.where(same, jnp.abs(rows - cols), 1000)
    first_half = lax.broadcasted_iota(jnp.int32, (1, 128), 1) < LEV

    def build(j):
        width = jnp.where(first_half, bands_ref[0, 2 * j] + 1, bands_ref[0, 2 * j + 1] + 1)
        tent = jnp.maximum(width - distance, 0).astype(F32).astype(BF16)
        wide = width.astype(F32)
        scale = 1.0 / (wide * wide)
        square = jnp.dot(tent, tent, preferred_element_type=F32) * (scale * scale)
        high = square.astype(BF16)
        tents[j] = tent
        sq_hi[j] = high
        sq_lo[j] = (square - high.astype(F32)).astype(BF16)
        inv2[j] = jnp.broadcast_to(scale, (8, 128))

    def build_some(step, carry):
        for extra in range(UNROLL):
            build(step * UNROLL + extra)
        return carry

    lax.fori_loop(0, PAIRS // UNROLL, build_some, 0)

    def restrict(fields):
        shares = [jnp.zeros((4, 16, 128), F32) for _ in range(5)]
        for parity in range(2):
            odd, even = fields(parity)
            total = jnp.zeros((4, 16, 128), F32)
            for t in range(4):
                total = total + ODD_TAPS[t] * odd[3 - t : 7 - t] + EVEN_TAPS[t] * even[3 - t : 7 - t]
            shares = [shares[k] + coef[parity, k][None] * total for k in range(5)]
        for k in range(5):
            gbuf[k] = shares[k]
        result = jnp.zeros((4, 8, 128), F32)
        for k in range(5):
            result = result + gbuf[k, :, 4 - k : 12 - k, :]
        return result

    def split_rows(parity, kind):
        at = pl.ds(4 + parity, 16, stride=2)
        return jnp.stack([wext[2 * b + kind, at, :] for b in range(7)])

    def fine_field(phase):
        def field(parity):
            along = jnp.zeros((10, 16, 128), F32)
            for k in range(5):
                along = along + coef[parity, k][None] * zext[phase, :, 4 + k : 20 + k, :]
            found = []
            for kind, taps in enumerate((ODD_TAPS, EVEN_TAPS)):
                total = taps[0] * along[0:7]
                for t in range(1, 4):
                    total = total + taps[t] * along[t : t + 7]
                found.append(wsplit[parity, kind] * total)
            return found

        return field

    first_lanes = lax.broadcasted_iota(jnp.int32, (4, 8, 128), 2) < LEV

    def split_pair(j, y):
        at = j * 256 if isinstance(j, int) else pl.multiple_of(j * 256, 256)
        e0 = ens[:, :, pl.ds(at, 128)].astype(F32)
        e1 = ens[:, :, pl.ds(at + 128, 128)].astype(F32)
        p0, p1 = e0 * y, e1 * y
        kept = jnp.where(first_lanes, p0, p1)
        moved = jnp.where(first_lanes, p1, p0)
        total = (kept + pltpu.roll(moved, LEV, 2)).reshape(32, 128)
        high = total.astype(BF16)
        low = (total - high.astype(F32)).astype(BF16)
        return e0, e1, high, low

    def combine_spread(y):
        acc = jnp.zeros((4, 8, 128), F32)
        for j in range(PAIRS):
            e0, e1, high, low = split_pair(j, y)
            both = jnp.concatenate([high, low], axis=0)
            main = jnp.dot(both, sq_hi[j], preferred_element_type=F32)
            rest = jnp.dot(high, sq_lo[j], preferred_element_type=F32)
            out = (main[:32] + (main[32:] + rest)).reshape(4, 8, 128)
            turned = pltpu.roll(out, LEV, 2)
            acc = acc + e0 * jnp.where(first_lanes, out, turned)
            acc = acc + e1 * jnp.where(first_lanes, turned, out)
        return acc

    def spread(which):
        y = yv[which]

        def body(step, carry):
            for extra in range(UNROLL):
                j = step * UNROLL + extra
                _, _, high, low = split_pair(j, y)
                both = jnp.concatenate([high, low], axis=0)
                main = jnp.dot(both, tents[j], preferred_element_type=F32)
                out = (main[:32] + main[32:]).reshape(4, 8, 128) * inv2[j][None]
                uvec[which, :, :, pl.ds(pl.multiple_of(j * 128, 128), 128)] = out
            return carry

        lax.fori_loop(0, PAIRS // UNROLL, body, 0)

    own_e.wait()
    for dlat, dlon in DIRECTIONS:
        inside(-dlat, lambda dlat=dlat, dlon=dlon: share_copy(dlat, dlon).wait_recv())
    start = ybuf[2:6, 8:16, :]
    for number in range(8):
        start = start + yin[number]
    yv[0] = start

    for phase in range(2):
        z = combine_spread(yv[phase])
        zext[phase, 3:7, 8:16, :] = z
        for dlat, dlon in DIRECTIONS:

            def send(dlat=dlat, dlon=dlon, phase=phase):
                z_copy(phase, dlat, dlon).start()

            inside(dlat, send)
        spread(phase)
        if phase == 0:
            for dlat in (-1, 1):
                inside(-dlat, lambda dlat=dlat: param_copy(dlat).wait_recv())
            find_coef((0, 1, 2))
            for dlat, dlon in DIRECTIONS:
                inside(-dlat, lambda dlat=dlat, dlon=dlon: weight_copy(dlat, dlon).wait_recv())
            for parity in range(2):
                for kind in range(2):
                    wsplit[parity, kind] = split_rows(parity, kind)
        for dlat, dlon in DIRECTIONS:

            def receive(dlat=dlat, dlon=dlon, phase=phase):
                z_copy(phase, dlat, dlon).wait_recv()

            inside(-dlat, receive)
        if phase == 0:
            yv[1] = restrict(fine_field(0))

    energy = jnp.zeros((16, 128), F32)
    for parity in range(2):
        along = jnp.zeros((8, 16, 128), F32)
        for k in range(5):
            along = along + coef[parity, k][None] * zext[1, 1:9, 4 + k : 20 + k, :]
        for kind, taps in enumerate((ODD_TAPS, EVEN_TAPS)):
            total = jnp.zeros((4, 16, 128), F32)
            for t in range(4):
                total = total + taps[t] * along[1 - kind + t : 5 - kind + t]
            weight = wsplit[parity, kind, 2 - kind : 6 - kind]
            energy = energy + jnp.sum(weight * total * total, axis=0)
    energy = jnp.where((row >= 2) & (row < 10), energy, 0.0)
    lane1 = lax.broadcasted_iota(jnp.int32, (1, 128), 1)
    planes = [
        jnp.sum(zext[left, 3:7, 8:16, :] * yv[right], axis=0)
        for left, right in ((0, 0), (0, 1), (1, 1))
    ] + [energy[0:8] + energy[8:16]]
    local = jnp.zeros((1, 128), F32)
    for number, plane in enumerate(planes):
        value = jnp.sum(jnp.sum(plane, axis=0, keepdims=True), axis=1, keepdims=True)
        local = local + jnp.where(lane1 == number, jnp.broadcast_to(value, (1, 128)), 0.0)

    for number, (me, count, device, slots, send_sems, recv_sems) in enumerate(stages):

        def stage_copy(target, slot):
            return pltpu.make_async_remote_copy(
                src_ref=slots.at[me],
                dst_ref=slots.at[slot],
                send_sem=send_sems.at[target],
                recv_sem=recv_sems.at[slot],
                device_id=device(target),
                device_id_type=MESH,
            )

        slots[me] = local
        for step in steps(count):
            stage_copy(lax.rem(me + step, count), me).start()
        if number == 0:
            yv[2] = restrict(fine_field(1))
            spread(2)
        for step in steps(count):
            other = lax.rem(me + step, count)
            stage_copy(other, other).wait_recv()
        local = slots[0]
        for slot in range(1, count):
            local = local + slots[slot]

    def picked(number):
        one = jnp.sum(jnp.where(lane1 == number, local, 0.0), axis=1, keepdims=True)
        return jnp.broadcast_to(one, (8, 128))

    a, b, d, f = (picked(number) for number in range(4))
    e = d
    square0 = a * (1.0 / entries) + EPSILON
    inverse0 = 1.0 / square0
    alpha0 = (a + b) * (inverse0 * (1.0 / entries))
    rest = 1.0 - alpha0
    own1 = (rest * (rest * a) + 2.0 * (rest * b) + d) * inverse0
    square1 = own1 * (1.0 / entries) + EPSILON
    inverse1 = 1.0 / square1
    mixed = (rest * (rest * b) + rest * (d + e) + f) * inverse0
    alpha1 = (own1 + mixed) * (inverse1 * (1.0 / entries))
    back = ((rest * a + b) + (rest * b + e)) * (inverse0 * (1.0 / entries))
    beta0, beta1 = jnp.sqrt(square0), jnp.sqrt(square1)
    q2 = jnp.sqrt(inverse0 * inverse1)
    q1 = (1.0 + rest - alpha1) * q2
    q0 = (rest - alpha1 * rest - back) * q2
    row8 = lax.broadcasted_iota(jnp.int32, (8, 128), 0)
    left = lax.broadcasted_iota(jnp.int32, (8, 128), 1) == 0
    table = jnp.where(row8 == 0, jnp.where(left, alpha0, alpha1), jnp.where(left, beta0, beta1))
    for number, q in enumerate((q0, q1, q2)):
        table = jnp.where(row8 == 2 + number, q, table)
    table_out[...] = table

    for dlat in (-1, 1):
        inside(dlat, lambda dlat=dlat: param_copy(dlat).wait_send())
    for dlat, dlon in DIRECTIONS:

        def drain(dlat=dlat, dlon=dlon):
            share_copy(dlat, dlon).wait_send()
            weight_copy(dlat, dlon).wait_send()
            z_copy(0, dlat, dlon).wait_send()
            z_copy(1, dlat, dlon).wait_send()

        inside(dlat, drain)
    for me, count, device, slots, send_sems, recv_sems in stages:
        for step in steps(count):
            target = lax.rem(me + step, count)
            pltpu.make_async_remote_copy(
                src_ref=slots.at[me],
                dst_ref=slots.at[me],
                send_sem=send_sems.at[target],
                recv_sem=recv_sems.at[me],
                device_id=device(target),
                device_id_type=MESH,
            ).wait_send()


def finish(table, u, coef_hbm, vec_hbm, corner, vec, sems):
    corner[...] = table[0:2, 0:2]
    tail = pltpu.make_async_copy(corner, coef_hbm, sems.at[4])
    tail.start()
    stores = [pltpu.make_async_copy(vec.at[c], vec_hbm.at[c], sems.at[c]) for c in range(4)]
    q = [jnp.broadcast_to(table[2 + k : 3 + k, :], (8, 128)) for k in range(3)]
    wide = [jnp.concatenate([part] * 8, axis=1) for part in q]
    for c in range(4):
        for step in range(M * LEV // 1024):
            at = slice(step * 1024, (step + 1) * 1024)
            vec[c, :, at] = (
                wide[0] * u[0, c, :, at] + wide[1] * u[1, c, :, at] + wide[2] * u[2, c, :, at]
            ).astype(BF16)
        stores[c].start()
    for store in stores:
        store.wait()
    tail.wait()


def per_device(topo, ensemble, innovation, obs_weight, lat_offset, lat_weight, band_widths):
    zh_n, x_n, zl_n, y_n, core_n = topo
    entries = float(4 * 8 * M * LEV * zh_n * x_n * zl_n * y_n * core_n)
    vmem = pltpu.VMEM
    dma = pltpu.SemaphoreType.DMA
    group_a, group_b, group_c = x_n * core_n, y_n, zh_n * zl_n
    anywhere = pl.BlockSpec(memory_space=pl.ANY)
    in_vmem = pl.BlockSpec(memory_space=pltpu.VMEM)
    table, u = pl.pallas_call(
        functools.partial(kernel, topo, entries),
        out_shape=(
            jax.ShapeDtypeStruct((8, 128), F32),
            jax.ShapeDtypeStruct((3, 4, 8, M * LEV), F32),
        ),
        in_specs=[
            anywhere,
            anywhere,
            anywhere,
            anywhere,
            anywhere,
            anywhere,
        ],
        out_specs=(in_vmem, in_vmem),
        scratch_shapes=[
            vmem((1, 16), jnp.int32),
            vmem((1, 16), F32),
            pltpu.SMEM((1, M), jnp.int32),
            vmem((4, 8, 2 * M * LEV), BF16),
            vmem((8, 16, 128), F32),
            vmem((8, 40, 128), F32),
            vmem((5, 8, 32, 128), F32),
            vmem((8, 24, 128), F32),
            vmem((8, 4, 8, 128), F32),
            vmem((8, 16, 128), F32),
            vmem((14, 40, 128), F32),
            vmem((2, 2, 7, 16, 128), F32),
            vmem((2, 10, 24, 128), F32),
            vmem((3, 4, 8, 128), F32),
            vmem((3, 8, 128), F32),
            vmem((2, 5, 16, 128), F32),
            vmem((5, 4, 16, 128), F32),
            vmem((PAIRS, 128, 128), BF16),
            vmem((PAIRS, 128, 128), BF16),
            vmem((PAIRS, 128, 128), BF16),
            vmem((PAIRS, 8, 128), F32),
            vmem((group_a, 1, 128), F32),
            vmem((group_b, 1, 128), F32),
            vmem((group_c, 1, 128), F32),
            dma((6,)),
            dma((2, 8)),
            dma((2, 8)),
            dma((2,)),
            dma((2,)),
            dma((2, 8)),
            dma((2, 8)),
            dma((group_a,)),
            dma((group_a,)),
            dma((group_b,)),
            dma((group_b,)),
            dma((group_c,)),
            dma((group_c,)),
        ],
        compiler_params=pltpu.CompilerParams(
            collective_id=0,
            has_side_effects=True,
            vmem_limit_bytes=24 * 1024 * 1024,
        ),
        name="lanczos",
    )(
        *(
            pltpu.with_memory_space_constraint(value, pltpu.HBM)
            for value in (
                ensemble,
                innovation,
                obs_weight,
                lat_offset.reshape(1, 16),
                lat_weight.reshape(1, 16),
                band_widths.reshape(1, M),
            )
        )
    )
    return pl.pallas_call(
        finish,
        out_shape=(
            jax.ShapeDtypeStruct((2, 2), F32),
            jax.ShapeDtypeStruct((4, 8, M * LEV), BF16),
        ),
        in_specs=[in_vmem, in_vmem],
        out_specs=(anywhere, anywhere),
        scratch_shapes=[
            vmem((2, 2), F32),
            vmem((4, 8, M * LEV), BF16),
            dma((5,)),
        ],
        compiler_params=pltpu.CompilerParams(vmem_limit_bytes=16 * 1024 * 1024),
        name="finish",
    )(table, u)


def solution(mesh):
    return jax.shard_map(
        functools.partial(per_device, TOPO),
        mesh=mesh,
        in_specs=(
            P("lon", "lat", None),
            P("lon", "lat", None),
            P("lon", "lat", None),
            P("lat"),
            P("lat"),
            P(),
        ),
        out_specs=(P(), P("lon", "lat", None)),
        check_vma=False,
    )
```
